256 devices in a mesh: tm: 64 (over y, z, core), pix: 2 (over x_lo), pb: 2 (over x_hi).
Axes of the slice: x: 4 (x_hi: 2, x_lo: 2; x = x_hi * 2 + x_lo), y: 4, z: 8, core: 2. Of those that a mesh axis runs over, the one named last changes fastest.
Arguments:
- frames: bfloat16 [2, 4096, 65536], P('pb', 'tm', 'pix'), may hold values from 0.05 to 15, as said below
- annulus_label: int32 [2, 65536], P('pb', 'pix'), may hold values from 0 to 3, as said below
- lag_width: int32 [2, 4], P('pb'), may hold values from 32 to 128, as said below
Outputs:
- correlation: float32 [2, 4, 4096, 128], P('pb', None, 'tm', 'pix')
The draws below stay inside these ranges and needn't reach their ends.
Inputs may be any that keep to these rules, and one draw needn't show every extreme that they name: `frames`: intensities are positive. `annulus_label`: each annulus label is held by exactly 16384 pixels of every band. `lag_width`: some entry equals 128 in every draw.
All inputs are finite; a program needn't handle non-finite values.
Results may differ from the reference program's by a relative error of at most 0.0003.
Values may be sent and summed in bfloat16 or wider, within the bound.
A program may use at most 64 MiB of HBM per device.

```python
import math
import jax
import jax.numpy as jnp
from jax import lax

F_DEV = 64
DELAYS_STORED = 128
PIX = 65536
RADII_IN_GROUP = 4
GROUP_NUMBER = 2
IMAGES_OVERALL = 4096


def annulus_order(key):
    labels = []
    for band_index in range(GROUP_NUMBER):
        order = jax.random.permutation(jax.random.fold_in(key, 101 + band_index), PIX).astype(jnp.int32)
        labels.append(order * RADII_IN_GROUP // PIX)
    return jnp.stack(labels, axis=0).astype(jnp.int32)


def complex_noise(key):
    return jax.random.normal(key, (2, GROUP_NUMBER, PIX), jnp.float32) * math.sqrt(0.5)


def draw_frames(key, part):
    labels = annulus_order(key)
    stochastic_seeds = [jax.random.fold_in(key, 300 + offset) for offset in range(8)]
    profile = 3.0 ** (jnp.arange(PIX, dtype=jnp.float32) / (PIX - 1))
    decay_base = jnp.exp(jax.random.uniform(stochastic_seeds[0], (GROUP_NUMBER, RADII_IN_GROUP), jnp.float32, 0.0, math.log(8.0)))
    phase_shift = jax.random.uniform(stochastic_seeds[1], (GROUP_NUMBER, RADII_IN_GROUP), jnp.float32, 0.0, 2.0 * math.pi)
    frame_time = jnp.arange(IMAGES_OVERALL, dtype=jnp.float32)[:, None, None]
    relaxation_interval = decay_base * jnp.exp(0.6 * jnp.sin(2.0 * math.pi * frame_time / (4.0 * DELAYS_STORED) + phase_shift))
    flare_onset = jax.random.randint(stochastic_seeds[2], (IMAGES_OVERALL, GROUP_NUMBER, RADII_IN_GROUP), 0, DELAYS_STORED) == 0
    flare_persist = jax.random.uniform(stochastic_seeds[3], (IMAGES_OVERALL, GROUP_NUMBER, RADII_IN_GROUP), jnp.float32, 0.45, 0.9)
    inherited_speed = jnp.exp(-1.0 / relaxation_interval) * jnp.where(flare_onset, flare_persist, 1.0)
    background = 0.4
    frame_scale = jnp.ones((IMAGES_OVERALL, GROUP_NUMBER, 1), jnp.float32)
    field_start = complex_noise(stochastic_seeds[6])

    def advance(speckle, inputs):
        frame_index, rate_now, scale_now = inputs
        rate_pixel = jnp.take_along_axis(rate_now, labels, axis=1)
        fresh = complex_noise(jax.random.fold_in(stochastic_seeds[7], frame_index))
        speckle = rate_pixel * speckle + jnp.sqrt(1.0 - rate_pixel * rate_pixel) * fresh
        observed = speckle
        speckle_power = jnp.minimum(observed[0] * observed[0] + observed[1] * observed[1], 6.0)
        intensity = profile * (background + (1.0 - background) * speckle_power) * scale_now
        return (speckle, intensity.astype(jnp.bfloat16))
    final_field, stacked = lax.scan(advance, field_start, (jnp.arange(IMAGES_OVERALL, dtype=jnp.int32), inherited_speed, frame_scale))
    return jnp.transpose(stacked, (1, 0, 2))


def draw_annulus_label(key, part):
    return annulus_order(key)


def draw_lag_width(key, part):
    key_width, key_pick = jax.random.split(jax.random.fold_in(key, 7))
    widths = jax.random.randint(key_width, (GROUP_NUMBER * RADII_IN_GROUP,), DELAYS_STORED // 4, DELAYS_STORED + 1).astype(jnp.int32)
    picked = jax.random.randint(key_pick, (), 0, GROUP_NUMBER * RADII_IN_GROUP).astype(jnp.int32)
    widths = jnp.where(jnp.arange(GROUP_NUMBER * RADII_IN_GROUP, dtype=jnp.int32) == picked, DELAYS_STORED, widths)
    return widths.reshape(GROUP_NUMBER, RADII_IN_GROUP).astype(jnp.int32)


def setup_inputs(seed: int = 0) -> dict:
    keys = jax.random.split(jax.random.key(seed), 4)
    return {
        "frames": draw_frames(jax.random.fold_in(keys[3], 71), 0),
        "annulus_label": draw_annulus_label(jax.random.fold_in(keys[3], 71), 0),
        "lag_width": draw_lag_width(jax.random.fold_in(keys[3], 71), 0),
    }


def reference(frames, annulus_label, lag_width):
    band_count, frame_total, pixel_count = frames.shape
    labels = jnp.arange(RADII_IN_GROUP, dtype=jnp.int32)
    onehot = (annulus_label[:, None, :] == labels[None, :, None]).astype(jnp.float32)
    padded = jnp.concatenate([frames, jnp.zeros((band_count, DELAYS_STORED, pixel_count), frames.dtype)], axis=1)
    row_ids = jnp.arange(F_DEV, dtype=jnp.int32)[:, None]
    lag_ids = jnp.arange(DELAYS_STORED, dtype=jnp.int32)[None, :]
    annulus_size = PIX // RADII_IN_GROUP

    def one_block(step):
        start = (step * F_DEV).astype(jnp.int32)
        own_rows = lax.dynamic_slice_in_dim(frames, start, F_DEV, 1).astype(jnp.float32)
        columns = lax.dynamic_slice_in_dim(padded, start, F_DEV + DELAYS_STORED, 1).astype(jnp.float32)
        masked = own_rows[:, None, :, :] * onehot[:, :, None, :]
        tile_full = jnp.einsum("brtp,bsp->brts", masked, columns)
        banded = tile_full[:, :, row_ids, row_ids + lag_ids]
        col_sums = jnp.einsum("brp,bsp->brs", onehot, columns)
        own_sums = col_sums[:, :, :F_DEV][..., None]
        far_sums = col_sums[:, :, row_ids + lag_ids]
        global_rows = start + row_ids
        valid = (lag_ids[None, None] < lag_width[:, :, None, None]) & ((global_rows + lag_ids) < frame_total)[None, None]
        denominator = jnp.where(valid, own_sums * far_sums, 1.0)
        return jnp.where(valid, annulus_size * banded / denominator, 0.0)

    blocks = lax.map(one_block, jnp.arange(frame_total // F_DEV, dtype=jnp.int32))
    return blocks.transpose(1, 2, 0, 3, 4).reshape(band_count, RADII_IN_GROUP, frame_total, DELAYS_STORED)
```

```python
import functools

import jax
import jax.numpy as jnp
from jax import lax
from jax.experimental import pallas as pl
from jax.experimental.pallas import tpu as pltpu
from jax.sharding import PartitionSpec as P

MESH = pl.DeviceIdType.MESH
RADII = 4
CHUNK = 1024
ONES = 16


def over_rows(masks, block):
    groups = block.reshape(1, -1, 16, block.shape[-1])
    return (groups * masks[:, None]).reshape(-1, block.shape[-1])


def contract(rows, columns):
    return lax.dot_general(rows, columns, (((1,), (1,)), ((), ())), preferred_element_type=jnp.float32)


def skewed(tile):
    rows, width = tile.shape
    groups = [pltpu.roll(tile[g : g + 8], (width - g) % width, 1) for g in range(0, rows, 8)]
    tile = jnp.concatenate(groups, axis=0)
    row = lax.broadcasted_iota(jnp.int32, tile.shape, 0)
    for step in (1, 2, 4):
        tile = jnp.where(row & step != 0, pltpu.roll(tile, width - step, 1), tile)
    return tile


def joined(left, right, radius):
    width = left.shape[1] // RADII
    lanes = slice(radius // 2 * 2 * width, (radius // 2 + 1) * 2 * width)
    left, right = left[:, lanes], right[:, lanes]
    if radius % 2:
        left = pltpu.roll(left, width, 1)
    else:
        right = pltpu.roll(right, width, 1)
    lane = lax.broadcasted_iota(jnp.int32, left.shape, 1)
    return jnp.where(lane < width, left, right)


def kernel(
    n,
    annulus_size,
    frames_ref,
    label_ref,
    lag_ref,
    out_ref,
    ab,
    stream,
    label,
    mask,
    acc1,
    acc2,
    from_pix,
    sums,
    from_even,
    from_even_x0,
    from_next,
    left,
    right,
    weight,
    own_sem,
    stream_send,
    stream_recv,
    mate_send,
    mate_recv,
    early_send,
    early_recv,
    late_send,
    late_recv,
    extended,
):
    f, pixels = frames_ref.shape[1:]
    chunk = min(CHUNK, pixels // 4)
    chunks = pixels // chunk
    own_rows, mate_rows = slice(ONES, ONES + f), slice(ONES + f, ONES + 2 * f)

    me, x = lax.axis_index("tm"), lax.axis_index("pix")
    odd = lax.rem(me, 2)
    even = odd == 0
    mate = me + 1 - 2 * odd
    ahead, behind = lax.rem(me + 2, n), lax.rem(me + n - 2, n)
    target = lax.rem(me + n - 2 + 4 * odd, n)
    other = 1 - x

    def at(k):
        return pl.ds(pl.multiple_of(k * chunk, chunk), chunk)

    def send(src, dst, sems, tm, pix):
        return pltpu.make_async_remote_copy(
            src_ref=src, dst_ref=dst, send_sem=sems[0], recv_sem=sems[1], device_id={"tm": tm, "pix": pix}, device_id_type=MESH
        )

    def stream_copy(k):
        return send(
            frames_ref.at[0, :, at(k)], stream.at[:, at(k)], (stream_send.at[k], stream_recv.at[k]), target, x
        )

    def mate_copy(k):
        return send(frames_ref.at[0, :, at(k)], ab.at[mate_rows, at(k)], (mate_send.at[k], mate_recv.at[k]), mate, x)

    own_copy = pltpu.make_async_copy(frames_ref.at[0], ab.at[own_rows], own_sem.at[0])
    label_copy = pltpu.make_async_copy(label_ref, label, own_sem.at[1])

    def early(i):
        return early_send.at[i], early_recv.at[i]

    def late(i):
        return late_send.at[i], late_recv.at[i]

    pix_copies = [send(acc1.at[i], from_pix.at[i], early(i), me, other) for i in range(2)]
    sums_back = send(sums.at[0], sums.at[2], early(2), behind, x)
    sums_mate_odd = send(sums.at[0], sums.at[1], early(3), mate, x)
    sums_mate_even = send(sums.at[2], sums.at[1], early(3), mate, x)
    ac_copy = send(acc2.at[0:f], from_even_x0, late(0), me, other)

    def bc_copy(x_from, x_to, way):
        return pltpu.make_async_remote_copy(
            src_ref=acc2.at[f : 2 * f],
            dst_ref=from_even.at[x_from],
            send_sem=late_send.at[way],
            recv_sem=late_recv.at[x_from + 1],
            device_id={"tm": mate, "pix": x_to},
            device_id_type=MESH,
        )

    def bd_copy(x_from):
        return pltpu.make_async_remote_copy(
            src_ref=acc2.at[0:f],
            dst_ref=from_next.at[x_from],
            send_sem=late_send.at[3],
            recv_sem=late_recv.at[3 + x_from],
            device_id={"tm": behind, "pix": 1},
            device_id_type=MESH,
        )

    own_copy.start()
    label_copy.start()
    barrier = pltpu.get_barrier_semaphore()
    for tm, pix in ((ahead, x), (behind, x), (mate, x), (me, other)):
        pl.semaphore_signal(barrier, inc=1, device_id={"tm": tm, "pix": pix}, device_id_type=MESH)
    pl.semaphore_wait(barrier, 4)

    @pl.loop(0, chunks)
    def _(k):
        stream_copy(k).start()

    @pl.when(odd == 1)
    def _():
        @pl.loop(0, chunks)
        def _(k):
            mate_copy(k).start()

    for tm, pix in ((mate, x), (me, other)):
        pl.semaphore_signal(extended, inc=1, device_id={"tm": tm, "pix": pix}, device_id_type=MESH)

    label_copy.wait()
    acc1[...] = jnp.zeros_like(acc1)
    acc2[...] = jnp.zeros_like(acc2)
    ab[0:ONES, :] = jnp.ones((ONES, pixels), jnp.bfloat16)

    @pl.loop(0, chunks)
    def _(k):
        labels = jnp.broadcast_to(label[:, at(k)], (16, chunk))
        for a in range(RADII):
            mask[a, :, at(k)] = jnp.where(labels == a, 1.0, 0.0).astype(jnp.bfloat16)

    own_copy.wait()

    @pl.loop(0, chunks)
    def _(k):
        masks = mask[:, :, at(k)]
        acc1[0] += contract(ab[0 : ONES + f, at(k)], over_rows(masks, ab[own_rows, at(k)]))

    pix_copies[0].start()

    @pl.when(even)
    def _():
        @pl.loop(0, chunks)
        def _(k):
            mate_copy(k).wait_recv()
            masks = mask[:, :, at(k)]
            acc1[1] += contract(ab[0 : ONES + f, at(k)], over_rows(masks, ab[mate_rows, at(k)]))

        pix_copies[1].start()

    def streamed(start, stop):
        @pl.when(even)
        def _():
            @pl.loop(start, stop)
            def _(k):
                stream_copy(k).wait_recv()
                columns = over_rows(mask[:, :, at(k)], stream[:, at(k)])
                acc2[...] += contract(ab[ONES : ONES + 2 * f, at(k)], columns)

        @pl.when(odd == 1)
        def _():
            @pl.loop(start, stop)
            def _(k):
                stream_copy(k).wait_recv()
                columns = over_rows(mask[:, :, at(k)], ab[own_rows, at(k)])
                acc2[0:f] += contract(stream[:, at(k)], columns)

    streamed(0, chunks // 4)
    pix_copies[0].wait()
    sums[0] = acc1[0, 0:8] + from_pix[0, 0:8]
    sums_back.start()

    @pl.when(odd == 1)
    def _():
        sums_mate_odd.start()

    streamed(chunks // 4, chunks // 2)
    sums_back.wait()

    @pl.when(even)
    def _():
        sums_mate_even.start()
        pix_copies[1].wait()

    streamed(chunks // 2, 3 * chunks // 4)

    @pl.when(even)
    def _():
        sums_mate_even.wait()

    @pl.when(odd == 1)
    def _():
        sums_mate_odd.wait()

    row = lax.broadcasted_iota(jnp.int32, (f, 2 * f), 0)
    lane = lax.broadcasted_iota(jnp.int32, (f, 2 * f), 1)
    lag = x * f + lane
    inside = me * f + row + lag < n * f
    near, far = sums[x], sums[x + 1]
    for a in range(RADII):
        own = joined(sums[0], sums[0], a)[0:1]
        own = jnp.sum(jnp.where(row == lane, jnp.broadcast_to(own, (f, 2 * f)), 0.0), axis=1, keepdims=True)
        there = skewed(jnp.broadcast_to(joined(near, far, a)[0:1], (f, 2 * f)))
        valid = (lag < lag_ref[0, a]) & inside
        weight[a] = jnp.where(valid, annulus_size / (own * there), 0.0)

    @pl.when(even & (x == 0))
    def _():
        left[...] = acc1[0, own_rows] + from_pix[0, own_rows]
        right[...] = acc1[1, own_rows] + from_pix[1, own_rows]

    @pl.when(even & (x == 1))
    def _():
        left[...] = acc1[1, own_rows] + from_pix[1, own_rows]

    @pl.when((odd == 1) & (x == 0))
    def _():
        left[...] = acc1[0, own_rows] + from_pix[0, own_rows]

    pl.semaphore_wait(extended, 2)
    streamed(3 * chunks // 4, chunks)

    @pl.when(even)
    def _():
        @pl.when(x == 0)
        def _():
            ac_copy.start()

        bc_copy(x, other, 1).start()
        bc_copy(x, x, 2).start()

        @pl.when(x == 1)
        def _():
            ac_copy.wait_recv()
            right[...] = acc2[0:f] + from_even_x0[...]

    @pl.when(odd == 1)
    def _():
        bd_copy(x).start()
        bc_copy(0, 0, 1).wait_recv()
        bc_copy(1, 0, 1).wait_recv()

        @pl.when(x == 0)
        def _():
            right[...] = from_even[0] + from_even[1]

        @pl.when(x == 1)
        def _():
            left[...] = from_even[0] + from_even[1]
            bd_copy(0).wait_recv()
            bd_copy(1).wait_recv()
            right[...] = from_next[0] + from_next[1]

    for a in range(RADII):
        out_ref[0, a] = (skewed(joined(left[...], right[...], a)) * weight[a])[:, 0:f]

    @pl.loop(0, chunks)
    def _(k):
        stream_copy(k).wait_send()

    @pl.when(odd == 1)
    def _():
        @pl.loop(0, chunks)
        def _(k):
            mate_copy(k).wait_send()

        bd_copy(x).wait_send()

    @pl.when(even)
    def _():
        @pl.when(x == 0)
        def _():
            ac_copy.wait_send()

        bc_copy(x, other, 1).wait_send()
        bc_copy(x, x, 2).wait_send()


def solution(mesh):
    n = mesh.shape["tm"]

    def shards(frames, annulus_label, lag_width):
        _, f, pixels = frames.shape
        chunks = pixels // min(CHUNK, pixels // 4)
        annulus_size = pixels * mesh.shape["pix"] // RADII
        width = RADII * f
        any_space = pl.BlockSpec(memory_space=pl.ANY)
        dma = pltpu.SemaphoreType.DMA
        return pl.pallas_call(
            functools.partial(kernel, n, float(annulus_size)),
            out_shape=jax.ShapeDtypeStruct((1, RADII, f, f), jnp.float32),
            in_specs=[any_space, any_space, pl.BlockSpec(memory_space=pltpu.SMEM)],
            out_specs=pl.BlockSpec(memory_space=pltpu.VMEM),
            scratch_shapes=[
                pltpu.VMEM((ONES + 2 * f, pixels), jnp.bfloat16),
                pltpu.VMEM((f, pixels), jnp.bfloat16),
                pltpu.VMEM((1, pixels), jnp.int32),
                pltpu.VMEM((RADII, 16, pixels), jnp.bfloat16),
                pltpu.VMEM((2, ONES + f, width), jnp.float32),
                pltpu.VMEM((2 * f, width), jnp.float32),
                pltpu.VMEM((2, ONES + f, width), jnp.float32),
                pltpu.VMEM((3, 8, width), jnp.float32),
                pltpu.VMEM((2, f, width), jnp.float32),
                pltpu.VMEM((f, width), jnp.float32),
                pltpu.VMEM((2, f, width), jnp.float32),
                pltpu.VMEM((f, width), jnp.float32),
                pltpu.VMEM((f, width), jnp.float32),
                pltpu.VMEM((RADII, f, 2 * f), jnp.float32),
                dma((2,)),
                dma((chunks,)),
                dma((chunks,)),
                dma((chunks,)),
                dma((chunks,)),
                dma((4,)),
                dma((4,)),
                dma((4,)),
                dma((5,)),
                pltpu.SemaphoreType.REGULAR,
            ],
            compiler_params=pltpu.CompilerParams(collective_id=0, has_side_effects=True),
            name="two_time",
        )(frames, annulus_label, lag_width)

    return jax.shard_map(
        shards,
        mesh=mesh,
        in_specs=(P("pb", "tm", "pix"), P("pb", "pix"), P("pb", None)),
        out_specs=P("pb", None, "tm", "pix"),
        check_vma=False,
    )
```

```python
import functools

import jax
import jax.numpy as jnp
from jax import lax
from jax.experimental import pallas as pl
from jax.experimental.pallas import tpu as pltpu
from jax.sharding import PartitionSpec as P

MESH = pl.DeviceIdType.MESH
RADII = 4
CHUNK = 1024
PIECE = 4
ONES = 16


def pieces_of(pixels):
    chunk = min(CHUNK, pixels // 16)
    big = pixels // (chunk * PIECE) - 1
    first = big * PIECE
    return chunk, big, ((first, 2), (first + 2, 1), (first + 3, 1))


def over_rows(masks, block):
    groups = block.reshape(1, -1, 16, block.shape[-1])
    return (groups * masks[:, None]).reshape(-1, block.shape[-1])


def contract(rows, columns):
    return lax.dot_general(rows, columns, (((1,), (1,)), ((), ())), preferred_element_type=jnp.float32)


def skewed(tile):
    rows, width = tile.shape
    groups = [pltpu.roll(tile[g : g + 8], (width - g) % width, 1) for g in range(0, rows, 8)]
    tile = jnp.concatenate(groups, axis=0)
    row = lax.broadcasted_iota(jnp.int32, tile.shape, 0)
    for step in (1, 2, 4):
        tile = jnp.where(row & step != 0, pltpu.roll(tile, width - step, 1), tile)
    return tile


def joined(left, right, radius):
    width = left.shape[1] // RADII
    lanes = slice(radius // 2 * 2 * width, (radius // 2 + 1) * 2 * width)
    left, right = left[:, lanes], right[:, lanes]
    if radius % 2:
        left = pltpu.roll(left, width, 1)
    else:
        right = pltpu.roll(right, width, 1)
    lane = lax.broadcasted_iota(jnp.int32, left.shape, 1)
    return jnp.where(lane < width, left, right)


def kernel(
    n,
    annulus_size,
    frames_ref,
    label_ref,
    lag_ref,
    out_ref,
    ab,
    stream,
    label,
    mask,
    acc1,
    acc2,
    from_pix,
    sums,
    from_even,
    from_even_x0,
    from_next,
    left,
    right,
    weight,
    widths,
    own_sem,
    stream_send,
    stream_recv,
    mate_send,
    mate_recv,
    early_send,
    early_recv,
    late_send,
    late_recv,
    extended,
):
    f, pixels = frames_ref.shape[1:]
    chunk, big, small = pieces_of(pixels)
    chunks = pixels // chunk
    held = big * 5 // 7
    own_rows, mate_rows = slice(ONES, ONES + f), slice(ONES + f, ONES + 2 * f)

    me, x = lax.axis_index("tm"), lax.axis_index("pix")
    odd = lax.rem(me, 2)
    even = odd == 0
    mate = me + 1 - 2 * odd
    ahead, behind = lax.rem(me + 2, n), lax.rem(me + n - 2, n)
    target = lax.rem(me + n - 2 + 4 * odd, n)
    other = 1 - x

    def at(k, count=1):
        return pl.ds(pl.multiple_of(k * chunk, chunk), chunk * count)

    def send(src, dst, sems, tm, pix):
        return pltpu.make_async_remote_copy(
            src_ref=src, dst_ref=dst, send_sem=sems[0], recv_sem=sems[1], device_id={"tm": tm, "pix": pix}, device_id_type=MESH
        )

    def stream_part(i, columns):
        return send(
            frames_ref.at[0, :, columns], stream.at[:, columns], (stream_send.at[i], stream_recv.at[i]), target, x
        )

    def stream_copy(k):
        return stream_part(k, at(k * PIECE, PIECE))

    small_copies = [stream_part(big + i, at(*place)) for i, place in enumerate(small)]

    def mate_copy(k):
        columns = at(k * PIECE, PIECE)
        return send(frames_ref.at[0, :, columns], ab.at[mate_rows, columns], (mate_send.at[k], mate_recv.at[k]), mate, x)

    own_copy = pltpu.make_async_copy(frames_ref.at[0], ab.at[own_rows], own_sem.at[0])
    label_copy = pltpu.make_async_copy(label_ref, label, own_sem.at[1])
    lag_copy = pltpu.make_async_copy(lag_ref, widths, own_sem.at[2])

    def early(i):
        return early_send.at[i], early_recv.at[i]

    def late(i):
        return late_send.at[i], late_recv.at[i]

    pix_copies = [send(acc1.at[i], from_pix.at[i], early(i), me, other) for i in range(2)]
    sums_back = send(sums.at[0], sums.at[2], early(2), behind, x)
    sums_mate_odd = send(sums.at[0], sums.at[1], early(3), mate, x)
    sums_mate_even = send(sums.at[2], sums.at[1], early(3), mate, x)
    ac_copy = send(acc2.at[0:f], from_even_x0, late(0), me, other)

    def bc_copy(x_from, x_to, way):
        return pltpu.make_async_remote_copy(
            src_ref=acc2.at[f : 2 * f],
            dst_ref=from_even.at[x_from],
            send_sem=late_send.at[way],
            recv_sem=late_recv.at[x_from + 1],
            device_id={"tm": mate, "pix": x_to},
            device_id_type=MESH,
        )

    def bd_copy(x_from):
        return pltpu.make_async_remote_copy(
            src_ref=acc2.at[0:f],
            dst_ref=from_next.at[x_from],
            send_sem=late_send.at[3],
            recv_sem=late_recv.at[3 + x_from],
            device_id={"tm": behind, "pix": 1},
            device_id_type=MESH,
        )

    barrier = pltpu.get_barrier_semaphore()
    for tm, pix in ((ahead, x), (behind, x), (mate, x), (me, other)):
        pl.semaphore_signal(barrier, inc=1, device_id={"tm": tm, "pix": pix}, device_id_type=MESH)
    pl.semaphore_wait(barrier, 4)

    @pl.loop(0, held)
    def _(k):
        stream_copy(k).start()

    label_copy.start()
    own_copy.start()
    lag_copy.start()

    @pl.when(odd == 1)
    def _():
        @pl.loop(0, big + 1)
        def _(k):
            mate_copy(k).start()

    for tm, pix in ((mate, x), (me, other)):
        pl.semaphore_signal(extended, inc=1, device_id={"tm": tm, "pix": pix}, device_id_type=MESH)

    acc1[...] = jnp.zeros_like(acc1)
    acc2[...] = jnp.zeros_like(acc2)
    ab[0:ONES, :] = jnp.ones((ONES, pixels), jnp.bfloat16)
    label_copy.wait()

    @pl.loop(0, chunks)
    def _(k):
        labels = jnp.broadcast_to(label[:, at(k)], (16, chunk))
        for a in range(RADII):
            mask[a, :, at(k)] = jnp.where(labels == a, 1.0, 0.0).astype(jnp.bfloat16)

    own_copy.wait()

    @pl.loop(0, chunks)
    def _(k):
        masks = mask[:, :, at(k)]
        acc1[0] += contract(ab[0 : ONES + f, at(k)], over_rows(masks, ab[own_rows, at(k)]))

    pix_copies[0].start()

    @pl.when(even)
    def _():
        @pl.loop(0, big + 1)
        def _(piece):
            mate_copy(piece).wait_recv()

            @pl.loop(piece * PIECE, piece * PIECE + PIECE)
            def _(k):
                masks = mask[:, :, at(k)]
                acc1[1] += contract(ab[0 : ONES + f, at(k)], over_rows(masks, ab[mate_rows, at(k)]))

        pix_copies[1].start()

    pix_copies[0].wait()
    sums[0] = acc1[0, 0:8] + from_pix[0, 0:8]
    sums_back.start()

    @pl.when(odd == 1)
    def _():
        sums_mate_odd.start()

    @pl.loop(held, big)
    def _(k):
        stream_copy(k).start()

    for copy in small_copies:
        copy.start()

    def multiplied(start, stop):
        @pl.when(even)
        def _():
            @pl.loop(start, stop)
            def _(k):
                columns = over_rows(mask[:, :, at(k)], stream[:, at(k)])
                acc2[...] += contract(ab[ONES : ONES + 2 * f, at(k)], columns)

        @pl.when(odd == 1)
        def _():
            @pl.loop(start, stop)
            def _(k):
                columns = over_rows(mask[:, :, at(k)], ab[own_rows, at(k)])
                acc2[0:f] += contract(stream[:, at(k)], columns)

    @pl.loop(0, held)
    def _(piece):
        stream_copy(piece).wait_recv()
        multiplied(piece * PIECE, piece * PIECE + PIECE)

    sums_back.wait()

    @pl.when(even)
    def _():
        sums_mate_even.start()
        pix_copies[1].wait()
        sums_mate_even.wait()

    @pl.when(odd == 1)
    def _():
        sums_mate_odd.wait()

    lag_copy.wait()
    row = lax.broadcasted_iota(jnp.int32, (f, 2 * f), 0)
    lane = lax.broadcasted_iota(jnp.int32, (f, 2 * f), 1)
    lag = x * f + lane
    inside = me * f + row + lag < n * f
    near, far = sums[x], sums[x + 1]
    for a in range(RADII):
        own = joined(sums[0], sums[0], a)[0:1]
        own = jnp.sum(jnp.where(row == lane, jnp.broadcast_to(own, (f, 2 * f)), 0.0), axis=1, keepdims=True)
        there = skewed(jnp.broadcast_to(joined(near, far, a)[0:1], (f, 2 * f)))
        valid = (lag < widths[0, a]) & inside
        weight[a] = jnp.where(valid, annulus_size / (own * there), 0.0)

    @pl.when(even & (x == 0))
    def _():
        left[...] = acc1[0, own_rows] + from_pix[0, own_rows]
        right[...] = acc1[1, own_rows] + from_pix[1, own_rows]

    @pl.when(even & (x == 1))
    def _():
        left[...] = acc1[1, own_rows] + from_pix[1, own_rows]

    @pl.when((odd == 1) & (x == 0))
    def _():
        left[...] = acc1[0, own_rows] + from_pix[0, own_rows]

    pl.semaphore_wait(extended, 2)

    @pl.loop(held, big)
    def _(piece):
        stream_copy(piece).wait_recv()
        multiplied(piece * PIECE, piece * PIECE + PIECE)

    for copy, (first, count) in zip(small_copies, small):
        copy.wait_recv()
        multiplied(first, first + count)

    @pl.when(even)
    def _():
        @pl.when(x == 0)
        def _():
            ac_copy.start()

        bc_copy(x, other, 1).start()
        bc_copy(x, x, 2).start()

        @pl.when(x == 1)
        def _():
            ac_copy.wait_recv()
            right[...] = acc2[0:f] + from_even_x0[...]

    @pl.when(odd == 1)
    def _():
        bd_copy(x).start()
        bc_copy(0, 0, 1).wait_recv()
        bc_copy(1, 0, 1).wait_recv()

        @pl.when(x == 0)
        def _():
            right[...] = from_even[0] + from_even[1]

        @pl.when(x == 1)
        def _():
            left[...] = from_even[0] + from_even[1]
            bd_copy(0).wait_recv()
            bd_copy(1).wait_recv()
            right[...] = from_next[0] + from_next[1]

    for a in range(RADII):
        out_ref[0, a] = (skewed(joined(left[...], right[...], a)) * weight[a])[:, 0:f]

    @pl.loop(0, big)
    def _(k):
        stream_copy(k).wait_send()

    for copy in small_copies:
        copy.wait_send()

    @pl.when(odd == 1)
    def _():
        @pl.loop(0, big + 1)
        def _(k):
            mate_copy(k).wait_send()

        bd_copy(x).wait_send()

    @pl.when(even)
    def _():
        @pl.when(x == 0)
        def _():
            ac_copy.wait_send()

        bc_copy(x, other, 1).wait_send()
        bc_copy(x, x, 2).wait_send()


def solution(mesh):
    n = mesh.shape["tm"]

    def shards(frames, annulus_label, lag_width):
        _, f, pixels = frames.shape
        _, big, small = pieces_of(pixels)
        parts = big + len(small)
        annulus_size = pixels * mesh.shape["pix"] // RADII
        width = RADII * f
        any_space = pl.BlockSpec(memory_space=pl.ANY)
        dma = pltpu.SemaphoreType.DMA
        return pl.pallas_call(
            functools.partial(kernel, n, float(annulus_size)),
            out_shape=pltpu.VMEM((1, RADII, f, f), jnp.float32),
            in_specs=[any_space] * 3,
            out_specs=pl.BlockSpec(memory_space=pltpu.VMEM),
            scratch_shapes=[
                pltpu.VMEM((ONES + 2 * f, pixels), jnp.bfloat16),
                pltpu.VMEM((f, pixels), jnp.bfloat16),
                pltpu.VMEM((1, pixels), jnp.int32),
                pltpu.VMEM((RADII, 16, pixels), jnp.bfloat16),
                pltpu.VMEM((2, ONES + f, width), jnp.float32),
                pltpu.VMEM((2 * f, width), jnp.float32),
                pltpu.VMEM((2, ONES + f, width), jnp.float32),
                pltpu.VMEM((3, 8, width), jnp.float32),
                pltpu.VMEM((2, f, width), jnp.float32),
                pltpu.VMEM((f, width), jnp.float32),
                pltpu.VMEM((2, f, width), jnp.float32),
                pltpu.VMEM((f, width), jnp.float32),
                pltpu.VMEM((f, width), jnp.float32),
                pltpu.VMEM((RADII, f, 2 * f), jnp.float32),
                pltpu.SMEM((1, RADII), jnp.int32),
                dma((3,)),
                dma((parts,)),
                dma((parts,)),
                dma((big + 1,)),
                dma((big + 1,)),
                dma((4,)),
                dma((4,)),
                dma((4,)),
                dma((5,)),
                pltpu.SemaphoreType.REGULAR,
            ],
            compiler_params=pltpu.CompilerParams(collective_id=0, has_side_effects=True),
            name="two_time",
        )(frames, annulus_label, lag_width)

    return jax.shard_map(
        shards,
        mesh=mesh,
        in_specs=(P("pb", "tm", "pix"), P("pb", "pix"), P("pb", None)),
        out_specs=P("pb", None, "tm", "pix"),
        check_vma=False,
    )
```

```python
import functools

import jax
import jax.numpy as jnp
from jax import lax
from jax.experimental import pallas as pl
from jax.experimental.pallas import tpu as pltpu
from jax.sharding import PartitionSpec as P

MESH = pl.DeviceIdType.MESH
RADII = 4
CHUNK = 1024
PIECE = 8
ONES = 16


def pieces_of(pixels):
    chunk = min(CHUNK, pixels // 32)
    piece = chunk * PIECE
    big = pixels // piece - 1
    first = big * piece
    small = ((first, piece // 2), (first + piece // 2, piece // 4), (first + piece * 3 // 4, piece // 8))
    return chunk, big, small + ((first + piece * 7 // 8, piece // 16), (first + piece * 15 // 16, piece // 16))


def over_rows(masks, block):
    groups = block.reshape(2, 1, -1, 16, block.shape[-1])
    return (groups * masks[None, :, None]).reshape(-1, block.shape[-1])


def contract(rows, columns):
    return lax.dot_general(rows, columns, (((1,), (1,)), ((), ())), preferred_element_type=jnp.float32)


def joined(left, right, radius, skew):
    width = left.shape[1] // 2
    quarter = width // RADII
    shape = (left.shape[0], width)
    place = lax.broadcasted_iota(jnp.int32, shape, 1)
    if skew:
        place = (place + lax.broadcasted_iota(jnp.int32, shape, 0)) & (width - 1)
    result = None
    for i in range(4):
        piece = (left, right)[i // 2][:, i % 2 * width : (i % 2 + 1) * width]
        lanes = (place + (radius - i) % 4 * quarter) & (width - 1)
        piece = jnp.take_along_axis(piece, lanes, axis=1)
        result = piece if result is None else jnp.where(place < i * quarter, result, piece)
    return result


def halves(f, below):
    lanes = RADII * f // 2
    first, second = slice(0, lanes), slice(lanes, 2 * lanes)
    if below:
        return ((0, f, first), (f // 2, f, second))
    return ((0, f, second), (0, f // 2, first))


def kernel(
    n,
    annulus_size,
    frames_ref,
    label_ref,
    lag_ref,
    out_ref,
    ab,
    stream,
    label,
    mask,
    acc1,
    acc2,
    from_pix,
    sums,
    from_even,
    from_even_x0,
    from_next,
    left,
    right,
    weight,
    widths,
    own_sem,
    stream_send,
    stream_recv,
    mate_send,
    mate_recv,
    early_send,
    early_recv,
    late_send,
    late_recv,
    extended,
    known,
):
    f, pixels = frames_ref.shape[1:]
    chunk, big, small = pieces_of(pixels)
    chunks = pixels // chunk
    held = 2
    own_rows, mate_rows = slice(ONES, ONES + f), slice(ONES + f, ONES + 2 * f)

    me, x = lax.axis_index("tm"), lax.axis_index("pix")
    odd = lax.rem(me, 2)
    even = odd == 0
    mate = me + 1 - 2 * odd
    ahead, behind = lax.rem(me + 2, n), lax.rem(me + n - 2, n)
    target = lax.rem(me + n - 2 + 4 * odd, n)
    source = lax.rem(me + n + 2 - 4 * odd, n)
    has_behind, has_ahead = me >= 2, me < n - 2
    sends = (even & has_behind) | ((odd == 1) & has_ahead)
    receives = (even & has_ahead) | ((odd == 1) & has_behind)
    other = 1 - x

    def at(k, count=1):
        return pl.ds(pl.multiple_of(k * chunk, chunk), chunk * count)

    def send(src, dst, sems, tm, pix):
        return pltpu.make_async_remote_copy(
            src_ref=src, dst_ref=dst, send_sem=sems[0], recv_sem=sems[1], device_id={"tm": tm, "pix": pix}, device_id_type=MESH
        )

    def stream_part(i, columns):
        return send(
            frames_ref.at[0, :, columns], stream.at[:, columns], (stream_send.at[i], stream_recv.at[i]), target, x
        )

    def stream_copy(k):
        return stream_part(k, at(k * PIECE, PIECE))

    small_copies = [stream_part(big + i, pl.ds(*place)) for i, place in enumerate(small)]

    def mate_copy(k):
        columns = at(k * PIECE, PIECE)
        return send(frames_ref.at[0, :, columns], ab.at[mate_rows, columns], (mate_send.at[k], mate_recv.at[k]), mate, x)

    own_copy = pltpu.make_async_copy(frames_ref.at[0], ab.at[own_rows], own_sem.at[0])
    label_copy = pltpu.make_async_copy(label_ref, label, own_sem.at[1])
    lag_copy = pltpu.make_async_copy(lag_ref, widths, own_sem.at[2])

    def early(i):
        return early_send.at[i], early_recv.at[i]

    def late(i):
        return late_send.at[i], late_recv.at[i]

    pix_copies = [send(acc1.at[i], from_pix.at[i], early(i), me, other) for i in range(2)]
    sums_back = send(sums.at[0], sums.at[2], early(2), behind, x)
    sums_mate_odd = send(sums.at[0], sums.at[1], early(3), mate, x)
    sums_mate_even = send(sums.at[2], sums.at[1], early(3), mate, x)
    def late_copies(base, dst, below, way, arrival, tm, pix):
        return [
            send(
                acc2.at[base + start : base + stop, lanes],
                dst.at[start:stop, lanes],
                (late_send.at[way + i], late_recv.at[arrival + i]),
                tm,
                pix,
            )
            for i, (start, stop, lanes) in enumerate(halves(f, below))
        ]

    ac_copies = late_copies(0, from_even_x0, True, 0, 0, me, 1)
    bc_copies = [
        [late_copies(f, from_even.at[i], j == 0, 2 + 2 * j, 2 + 2 * i, mate, j) for j in range(2)] for i in range(2)
    ]

    def bd_copies(x_from):
        return late_copies(0, from_next.at[x_from], True, 0, 6 + 2 * x_from, behind, 1)

    def each(copies, action):
        for copy in copies:
            getattr(copy, action)()

    def signal(semaphore, tm, pix):
        pl.semaphore_signal(semaphore, inc=1, device_id={"tm": tm, "pix": pix}, device_id_type=MESH)

    def one_if(condition):
        return jnp.where(condition, 1, 0).astype(jnp.int32)

    label_copy.start()
    own_copy.start()
    lag_copy.start()

    barrier = pltpu.get_barrier_semaphore()

    @pl.when(receives)
    def _():
        signal(barrier, source, x)

    signal(barrier, mate, x)
    signal(barrier, me, other)
    pl.semaphore_wait(barrier, 2 + one_if(sends))

    @pl.when(sends)
    def _():
        @pl.loop(0, held)
        def _(k):
            stream_copy(k).start()

        signal(known, target, x)

    @pl.when(odd == 1)
    def _():
        @pl.loop(0, big + 1)
        def _(k):
            mate_copy(k).start()

    @pl.when(~has_ahead)
    def _():
        sums[2] = jnp.zeros_like(sums[2])
        from_next[...] = jnp.zeros_like(from_next)

    acc1[...] = jnp.zeros_like(acc1)
    acc2[...] = jnp.zeros_like(acc2)
    ab[0:ONES, :] = jnp.ones((ONES, pixels), jnp.bfloat16)
    label_copy.wait()

    @pl.loop(0, chunks)
    def _(k):
        labels = jnp.broadcast_to(label[:, at(k)], (16, chunk))
        for a in range(RADII):
            mask[a, :, at(k)] = jnp.where(labels == a, 1.0, 0.0).astype(jnp.bfloat16)

    own_copy.wait()

    @pl.loop(0, chunks)
    def _(k):
        masks = mask[:, :, at(k)]
        acc1[0] += contract(ab[0 : ONES + f, at(k)], over_rows(masks, ab[own_rows, at(k)]))

    pix_copies[0].start()

    @pl.when(receives)
    def _():
        pl.semaphore_wait(known, 1)

    signal(extended, mate, x)
    signal(extended, me, other)

    @pl.when(even)
    def _():
        @pl.loop(0, big + 1)
        def _(piece):
            mate_copy(piece).wait_recv()

            @pl.loop(piece * PIECE, piece * PIECE + PIECE)
            def _(k):
                masks = mask[:, :, at(k)]
                acc1[1] += contract(ab[0 : ONES + f, at(k)], over_rows(masks, ab[mate_rows, at(k)]))

        pix_copies[1].start()

    pix_copies[0].wait()
    sums[0] = acc1[0, 0:8] + from_pix[0, 0:8]

    @pl.when(has_behind)
    def _():
        sums_back.start()

    @pl.when(odd == 1)
    def _():
        sums_mate_odd.start()

    @pl.when(sends)
    def _():
        @pl.loop(held, big)
        def _(k):
            stream_copy(k).start()

        for copy in small_copies:
            copy.start()

    def multiply(columns):
        @pl.when(even)
        def _():
            spread = over_rows(mask[:, :, columns], stream[:, columns])
            acc2[...] += contract(ab[ONES : ONES + 2 * f, columns], spread)

        @pl.when(odd == 1)
        def _():
            spread = over_rows(mask[:, :, columns], ab[own_rows, columns])
            acc2[0:f] += contract(stream[:, columns], spread)

    def multiply_piece(piece):
        stream_copy(piece).wait_recv()

        @pl.loop(piece * PIECE, piece * PIECE + PIECE)
        def _(k):
            multiply(at(k))

    @pl.when(receives)
    def _():
        pl.loop(0, held)(multiply_piece)

    @pl.when(has_ahead)
    def _():
        sums_back.wait_recv()

    @pl.when(has_behind)
    def _():
        sums_back.wait_send()

    @pl.when(even)
    def _():
        sums_mate_even.start()
        pix_copies[1].wait()
        sums_mate_even.wait()

    @pl.when(odd == 1)
    def _():
        sums_mate_odd.wait()

    lag_copy.wait()
    row = lax.broadcasted_iota(jnp.int32, (f, 2 * f), 0)
    lane = lax.broadcasted_iota(jnp.int32, (f, 2 * f), 1)
    lag = x * f + lane
    inside = me * f + row + lag < n * f
    near, far = sums[x, 0:1], sums[x + 1, 0:1]
    wide = (f, RADII * f)
    for a in range(RADII):
        own = joined(sums[0], sums[0], a, False)[0:1]
        own = jnp.sum(jnp.where(row == lane, jnp.broadcast_to(own, (f, 2 * f)), 0.0), axis=1, keepdims=True)
        there = joined(jnp.broadcast_to(near, wide), jnp.broadcast_to(far, wide), a, True)
        valid = (lag < widths[0, a]) & inside
        weight[a] = jnp.where(valid, annulus_size / (own * there), 0.0)

    @pl.when(even & (x == 0))
    def _():
        left[...] = acc1[0, own_rows] + from_pix[0, own_rows]
        right[...] = acc1[1, own_rows] + from_pix[1, own_rows]

    @pl.when(even & (x == 1))
    def _():
        left[...] = acc1[1, own_rows] + from_pix[1, own_rows]

    @pl.when((odd == 1) & (x == 0))
    def _():
        left[...] = acc1[0, own_rows] + from_pix[0, own_rows]

    pl.semaphore_wait(extended, 2)

    @pl.when(receives)
    def _():
        pl.loop(held, big)(multiply_piece)

        for copy, (first, count) in zip(small_copies, small):
            copy.wait_recv()
            step = min(chunk, count)

            @pl.loop(0, count // step)
            def _(k, first=first, step=step):
                multiply(pl.ds(pl.multiple_of(first + k * step, step), step))

    @pl.when(even)
    def _():
        @pl.when(x == 0)
        def _():
            each(bc_copies[0][1], "start")
            each(ac_copies, "start")
            each(bc_copies[0][0], "start")

        @pl.when(x == 1)
        def _():
            each(bc_copies[1][0], "start")
            each(bc_copies[1][1], "start")
            each(ac_copies, "wait_recv")
            right[...] = acc2[0:f] + from_even_x0[...]

    @pl.when(odd == 1)
    def _():
        @pl.when(has_behind)
        def _():
            each(bd_copies(x), "start")

        @pl.when(x == 0)
        def _():
            each(bc_copies[0][0] + bc_copies[1][0], "wait_recv")
            right[...] = from_even[0] + from_even[1]

        @pl.when(x == 1)
        def _():
            each(bc_copies[0][1] + bc_copies[1][1], "wait_recv")
            left[...] = from_even[0] + from_even[1]

            @pl.when(has_ahead)
            def _():
                each(bd_copies(0) + bd_copies(1), "wait_recv")

            right[...] = from_next[0] + from_next[1]

    for a in range(RADII):
        out_ref[0, a] = (joined(left[...], right[...], a, True) * weight[a])[:, 0:f]

    @pl.when(sends)
    def _():
        @pl.loop(0, big)
        def _(k):
            stream_copy(k).wait_send()

        for copy in small_copies:
            copy.wait_send()

    @pl.when(odd == 1)
    def _():
        @pl.loop(0, big + 1)
        def _(k):
            mate_copy(k).wait_send()

        @pl.when(has_behind)
        def _():
            each(bd_copies(x), "wait_send")

    @pl.when(even)
    def _():
        for i in range(2):

            @pl.when(x == i)
            def _(i=i):
                each(bc_copies[i][0] + bc_copies[i][1], "wait_send")

        @pl.when(x == 0)
        def _():
            each(ac_copies, "wait_send")


def solution(mesh):
    n = mesh.shape["tm"]

    def shards(frames, annulus_label, lag_width):
        _, f, pixels = frames.shape
        _, big, small = pieces_of(pixels)
        parts = big + len(small)
        annulus_size = pixels * mesh.shape["pix"] // RADII
        width = RADII * f
        any_space = pl.BlockSpec(memory_space=pl.ANY)
        dma = pltpu.SemaphoreType.DMA
        return pl.pallas_call(
            functools.partial(kernel, n, float(annulus_size)),
            out_shape=pltpu.VMEM((1, RADII, f, f), jnp.float32),
            in_specs=[any_space] * 3,
            out_specs=pl.BlockSpec(memory_space=pltpu.VMEM),
            scratch_shapes=[
                pltpu.VMEM((ONES + 2 * f, pixels), jnp.bfloat16),
                pltpu.VMEM((f, pixels), jnp.bfloat16),
                pltpu.VMEM((1, pixels), jnp.int32),
                pltpu.VMEM((RADII, 16, pixels), jnp.bfloat16),
                pltpu.VMEM((2, ONES + f, width), jnp.float32),
                pltpu.VMEM((2 * f, width), jnp.float32),
                pltpu.VMEM((2, ONES + f, width), jnp.float32),
                pltpu.VMEM((3, 8, width), jnp.float32),
                pltpu.VMEM((2, f, width), jnp.float32),
                pltpu.VMEM((f, width), jnp.float32),
                pltpu.VMEM((2, f, width), jnp.float32),
                pltpu.VMEM((f, width), jnp.float32),
                pltpu.VMEM((f, width), jnp.float32),
                pltpu.VMEM((RADII, f, 2 * f), jnp.float32),
                pltpu.SMEM((1, RADII), jnp.int32),
                dma((3,)),
                dma((parts,)),
                dma((parts,)),
                dma((big + 1,)),
                dma((big + 1,)),
                dma((4,)),
                dma((4,)),
                dma((6,)),
                dma((10,)),
                pltpu.SemaphoreType.REGULAR,
                pltpu.SemaphoreType.REGULAR,
            ],
            compiler_params=pltpu.CompilerParams(collective_id=0, has_side_effects=True),
            name="two_time",
        )(frames, annulus_label, lag_width)

    return jax.shard_map(
        shards,
        mesh=mesh,
        in_specs=(P("pb", "tm", "pix"), P("pb", "pix"), P("pb", None)),
        out_specs=P("pb", None, "tm", "pix"),
        check_vma=False,
    )
```

```python
import functools

import jax
import jax.numpy as jnp
from jax import lax
from jax.experimental import pallas as pl
from jax.experimental.pallas import tpu as pltpu
from jax.sharding import PartitionSpec as P

MESH = pl.DeviceIdType.MESH
RADII = 4
CHUNK = 1024
MATE_PIECES = 4
ONES = 16


def pieces_of(pixels):
    late, first, width = [], 0, pixels // 2
    while width >= pixels // 64:
        late.append((1, first, width))
        first, width = first + width, width // 2
    early = [(0, 0, pixels)]
    return early, late + [(1, first, pixels - first)]


def over_half(masks, rows):
    groups = rows.reshape(1, -1, 16, rows.shape[-1])
    return (groups * masks[:, None]).reshape(-1, rows.shape[-1])


def over_rows(masks, block):
    groups = block.reshape(2, 1, -1, 16, block.shape[-1])
    return (groups * masks[None, :, None]).reshape(-1, block.shape[-1])


def contract(rows, columns):
    return lax.dot_general(rows, columns, (((1,), (1,)), ((), ())), preferred_element_type=jnp.float32)


def joined(left, right, radius, skew):
    width = left.shape[1] // 2
    quarter = width // RADII
    shape = (left.shape[0], width)
    place = lax.broadcasted_iota(jnp.int32, shape, 1)
    if skew:
        place = (place + lax.broadcasted_iota(jnp.int32, shape, 0)) & (width - 1)
    result = None
    for i in range(4):
        piece = (left, right)[i // 2][:, i % 2 * width : (i % 2 + 1) * width]
        lanes = (place + (radius - i) % 4 * quarter) & (width - 1)
        piece = jnp.take_along_axis(piece, lanes, axis=1)
        result = piece if result is None else jnp.where(place < i * quarter, result, piece)
    return result


def needed(f, half, below):
    if below:
        return (0, f) if half == 0 else (f // 2, f)
    return (0, f // 2) if half == 0 else (0, f)


def kernel(
    n,
    annulus_size,
    frames_ref,
    label_ref,
    lag_ref,
    out_ref,
    ab,
    stream,
    label,
    mask,
    acc1,
    acc2,
    from_pix,
    sums,
    low,
    high,
    from_even,
    from_even_x0,
    from_next_low,
    from_next_high,
    left,
    right,
    weight,
    widths,
    own_sem,
    stream_send,
    stream_recv,
    mate_send,
    mate_recv,
    early_send,
    early_recv,
    late_send,
    late_recv,
    extended,
    known,
):
    f, pixels = frames_ref.shape[1:]
    early_pieces, late_pieces = pieces_of(pixels)
    chunk = min(CHUNK, pixels // 32)
    chunks, per_piece = pixels // chunk, pixels // chunk // MATE_PIECES
    h = f // 2
    tiles = (slice(0, RADII * h), slice(RADII * h, RADII * f))
    own_rows, mate_rows = slice(ONES, ONES + f), slice(ONES + f, ONES + 2 * f)

    me, x = lax.axis_index("tm"), lax.axis_index("pix")
    odd = lax.rem(me, 2)
    even = odd == 0
    mate = me + 1 - 2 * odd
    ahead, behind = lax.rem(me + 2, n), lax.rem(me + n - 2, n)
    target = lax.rem(me + n - 2 + 4 * odd, n)
    source = lax.rem(me + n + 2 - 4 * odd, n)
    has_behind, has_ahead = me >= 2, me < n - 2
    sends = (even & has_behind) | ((odd == 1) & has_ahead)
    receives = (even & has_ahead) | ((odd == 1) & has_behind)
    other = 1 - x

    def at(k, count=1):
        return pl.ds(pl.multiple_of(k * chunk, chunk), chunk * count)

    def send(src, dst, sems, tm, pix):
        return pltpu.make_async_remote_copy(
            src_ref=src, dst_ref=dst, send_sem=sems[0], recv_sem=sems[1], device_id={"tm": tm, "pix": pix}, device_id_type=MESH
        )

    stream_copies = [
        send(
            frames_ref.at[0, half * h : (half + 1) * h, pl.ds(first, width)],
            stream.at[half * h : (half + 1) * h, pl.ds(first, width)],
            (stream_send.at[i], stream_recv.at[i]),
            target,
            x,
        )
        for i, (half, first, width) in enumerate(early_pieces + late_pieces)
    ]
    early_copies, late_copies = stream_copies[: len(early_pieces)], stream_copies[len(early_pieces) :]

    def mate_copy(k):
        columns = at(k * per_piece, per_piece)
        return send(frames_ref.at[0, :, columns], ab.at[mate_rows, columns], (mate_send.at[k], mate_recv.at[k]), mate, x)

    own_copy = pltpu.make_async_copy(frames_ref.at[0], ab.at[own_rows], own_sem.at[0])
    label_copy = pltpu.make_async_copy(label_ref, label, own_sem.at[1])
    lag_copy = pltpu.make_async_copy(lag_ref, widths, own_sem.at[2])

    def early(i):
        return early_send.at[i], early_recv.at[i]

    def late(i):
        return late_send.at[i], late_recv.at[i]

    pix_copies = [send(acc1.at[i], from_pix.at[i], early(i), me, other) for i in range(2)]
    sums_back = send(sums.at[0], sums.at[2], early(2), behind, x)
    sums_mate_odd = send(sums.at[0], sums.at[1], early(3), mate, x)
    sums_mate_even = send(sums.at[2], sums.at[1], early(3), mate, x)
    def tile_copies(base, dst, below, way, arrival, tm, pix):
        copies = []
        for half in range(2):
            start, stop = needed(f, half, below)
            src = acc2.at[half, base + start : base + stop]
            sems = (late_send.at[way + half], late_recv.at[arrival + half])
            copies.append(send(src, dst.at[half, start:stop], sems, tm, pix))
        return copies

    ac_copies = tile_copies(0, from_even_x0, True, 0, 0, me, 1)
    bc_copies = [
        [tile_copies(f, from_even.at[i], j == 0, 2 + 2 * j, 2 + 2 * i, mate, j) for j in range(2)] for i in range(2)
    ]

    def bd_copies(x_from):
        return [
            send(src, dst.at[x_from], (late_send.at[i], late_recv.at[6 + 2 * x_from + i]), behind, 1)
            for i, (src, dst) in enumerate(((low, from_next_low), (high, from_next_high)))
        ]

    def exchange(half):
        @pl.when(even & (x == 0))
        def _():
            each([ac_copies[half], bc_copies[0][1][half], bc_copies[0][0][half]], "start")

        @pl.when(even & (x == 1))
        def _():
            each([bc_copies[1][0][half], bc_copies[1][1][half]], "start")

        if half == 1:

            @pl.when((odd == 1) & has_behind)
            def _():
                each(bd_copies(x)[::-1], "start")

    def gather(half):
        below, above = slice(*needed(f, half, True)), slice(*needed(f, half, False))

        @pl.when(even & (x == 1))
        def _():
            ac_copies[half].wait_recv()
            right[below, tiles[half]] = acc2[half, below] + from_even_x0[half, below]

        @pl.when((odd == 1) & (x == 0))
        def _():
            each([bc_copies[0][0][half], bc_copies[1][0][half]], "wait_recv")
            right[below, tiles[half]] = from_even[0, half, below] + from_even[1, half, below]

        @pl.when((odd == 1) & (x == 1))
        def _():
            each([bc_copies[0][1][half], bc_copies[1][1][half]], "wait_recv")
            left[above, tiles[half]] = from_even[0, half, above] + from_even[1, half, above]

        if half == 1:

            @pl.when((odd == 1) & (x == 1) & has_ahead)
            def _():
                each(bd_copies(0) + bd_copies(1), "wait_recv")
                right[0:h, tiles[0]] = from_next_low[0] + from_next_low[1]
                right[h:f] = from_next_high[0] + from_next_high[1]

    def each(copies, action):
        for copy in copies:
            getattr(copy, action)()

    def signal(semaphore, tm, pix):
        pl.semaphore_signal(semaphore, inc=1, device_id={"tm": tm, "pix": pix}, device_id_type=MESH)

    def one_if(condition):
        return jnp.where(condition, 1, 0).astype(jnp.int32)

    label_copy.start()
    own_copy.start()
    lag_copy.start()

    barrier = pltpu.get_barrier_semaphore()

    @pl.when(receives)
    def _():
        signal(barrier, source, x)

    signal(barrier, mate, x)
    signal(barrier, me, other)
    pl.semaphore_wait(barrier, 2 + one_if(sends))

    @pl.when(sends)
    def _():
        each(early_copies, "start")
        signal(known, target, x)

    @pl.when(odd == 1)
    def _():
        @pl.loop(0, MATE_PIECES)
        def _(k):
            mate_copy(k).start()

    @pl.when(~has_ahead)
    def _():
        sums[2] = jnp.zeros_like(sums[2])

    acc1[...] = jnp.zeros_like(acc1)
    for tile in (acc2, low, high, left, right):
        tile[...] = jnp.zeros_like(tile)

    ab[0:ONES, :] = jnp.ones((ONES, pixels), jnp.bfloat16)
    label_copy.wait()

    @pl.loop(0, chunks)
    def _(k):
        labels = jnp.broadcast_to(label[:, at(k)], (16, chunk))
        for a in range(RADII):
            mask[a, :, at(k)] = jnp.where(labels == a, 1.0, 0.0).astype(jnp.bfloat16)

    own_copy.wait()

    @pl.loop(0, chunks)
    def _(k):
        masks = mask[:, :, at(k)]
        acc1[0] += contract(ab[0 : ONES + f, at(k)], over_rows(masks, ab[own_rows, at(k)]))

    pix_copies[0].start()

    @pl.when(receives)
    def _():
        pl.semaphore_wait(known, 1)

    signal(extended, mate, x)
    signal(extended, me, other)

    @pl.when(even)
    def _():
        @pl.loop(0, MATE_PIECES)
        def _(piece):
            mate_copy(piece).wait_recv()

            @pl.loop(piece * per_piece, piece * per_piece + per_piece)
            def _(k):
                masks = mask[:, :, at(k)]
                acc1[1] += contract(ab[0 : ONES + f, at(k)], over_rows(masks, ab[mate_rows, at(k)]))

        pix_copies[1].start()

    pix_copies[0].wait()
    sums[0] = acc1[0, 0:8] + from_pix[0, 0:8]

    @pl.when(has_behind)
    def _():
        sums_back.start()

    @pl.when(odd == 1)
    def _():
        sums_mate_odd.start()

    @pl.when(sends)
    def _():
        each(late_copies, "start")

    def multiply(half, columns):
        rows = slice(half * h, (half + 1) * h)

        @pl.when(even)
        def _():
            spread = over_half(mask[:, :, columns], stream[rows, columns])
            first = needed(f, half, True)[0]
            acc2[half, first : 2 * f] += contract(ab[ONES + first : ONES + 2 * f, columns], spread)

        @pl.when(odd == 1)
        def _():
            if half == 0:
                spread = over_half(mask[:, :, columns], ab[ONES : ONES + h, columns])
                low[...] += contract(stream[rows, columns], spread)
            else:
                spread = over_rows(mask[:, :, columns], ab[own_rows, columns])
                high[...] += contract(stream[rows, columns], spread)

    def multiply_all(copies, pieces):
        @pl.when(receives)
        def _():
            for copy, (half, first, width) in zip(copies, pieces):
                copy.wait_recv()
                step = min(chunk, width)

                @pl.loop(0, width // step)
                def _(k, half=half, first=first, step=step):
                    multiply(half, pl.ds(pl.multiple_of(first + k * step, step), step))

    multiply_all(early_copies, early_pieces)
    pl.semaphore_wait(extended, 2)
    exchange(0)

    @pl.when(has_ahead)
    def _():
        sums_back.wait_recv()

    @pl.when(has_behind)
    def _():
        sums_back.wait_send()

    @pl.when(even)
    def _():
        sums_mate_even.start()
        pix_copies[1].wait()
        sums_mate_even.wait()

    @pl.when(odd == 1)
    def _():
        sums_mate_odd.wait()

    lag_copy.wait()
    row = lax.broadcasted_iota(jnp.int32, (f, 2 * f), 0)
    lane = lax.broadcasted_iota(jnp.int32, (f, 2 * f), 1)
    lag = x * f + lane
    inside = me * f + row + lag < n * f
    near, far = sums[x, 0:1], sums[x + 1, 0:1]
    wide = (f, RADII * f)
    for a in range(RADII):
        own = joined(sums[0], sums[0], a, False)[0:1]
        own = jnp.sum(jnp.where(row == lane, jnp.broadcast_to(own, (f, 2 * f)), 0.0), axis=1, keepdims=True)
        there = joined(jnp.broadcast_to(near, wide), jnp.broadcast_to(far, wide), a, True)
        valid = (lag < widths[0, a]) & inside
        weight[a] = jnp.where(valid, annulus_size / (own * there), 0.0)

    @pl.when(even & (x == 0))
    def _():
        left[...] = acc1[0, own_rows] + from_pix[0, own_rows]
        right[...] = acc1[1, own_rows] + from_pix[1, own_rows]

    @pl.when(even & (x == 1))
    def _():
        left[...] = acc1[1, own_rows] + from_pix[1, own_rows]

    @pl.when((odd == 1) & (x == 0))
    def _():
        left[...] = acc1[0, own_rows] + from_pix[0, own_rows]

    multiply_all(late_copies[:1], late_pieces[:1])
    gather(0)
    multiply_all(late_copies[1:], late_pieces[1:])
    exchange(1)
    gather(1)

    for a in range(RADII):
        out_ref[0, a] = (joined(left[...], right[...], a, True) * weight[a])[:, 0:f]

    @pl.when(sends)
    def _():
        each(stream_copies, "wait_send")

    @pl.when(odd == 1)
    def _():
        @pl.loop(0, MATE_PIECES)
        def _(k):
            mate_copy(k).wait_send()

        @pl.when(has_behind)
        def _():
            each(bd_copies(x), "wait_send")

    @pl.when(even)
    def _():
        for i in range(2):

            @pl.when(x == i)
            def _(i=i):
                each(bc_copies[i][0] + bc_copies[i][1], "wait_send")

        @pl.when(x == 0)
        def _():
            each(ac_copies, "wait_send")


def solution(mesh):
    n = mesh.shape["tm"]

    def shards(frames, annulus_label, lag_width):
        _, f, pixels = frames.shape
        parts = sum(map(len, pieces_of(pixels)))
        h = f // 2
        annulus_size = pixels * mesh.shape["pix"] // RADII
        width = RADII * f
        any_space = pl.BlockSpec(memory_space=pl.ANY)
        dma = pltpu.SemaphoreType.DMA
        return pl.pallas_call(
            functools.partial(kernel, n, float(annulus_size)),
            out_shape=pltpu.VMEM((1, RADII, f, f), jnp.float32),
            in_specs=[any_space] * 3,
            out_specs=pl.BlockSpec(memory_space=pltpu.VMEM),
            scratch_shapes=[
                pltpu.VMEM((ONES + 2 * f, pixels), jnp.bfloat16),
                pltpu.VMEM((f, pixels), jnp.bfloat16),
                pltpu.VMEM((1, pixels), jnp.int32),
                pltpu.VMEM((RADII, 16, pixels), jnp.bfloat16),
                pltpu.VMEM((2, ONES + f, width), jnp.float32),
                pltpu.VMEM((2, 2 * f, width // 2), jnp.float32),
                pltpu.VMEM((2, ONES + f, width), jnp.float32),
                pltpu.VMEM((3, 8, width), jnp.float32),
                pltpu.VMEM((h, width // 2), jnp.float32),
                pltpu.VMEM((h, width), jnp.float32),
                pltpu.VMEM((2, 2, f, width // 2), jnp.float32),
                pltpu.VMEM((2, f, width // 2), jnp.float32),
                pltpu.VMEM((2, h, width // 2), jnp.float32),
                pltpu.VMEM((2, h, width), jnp.float32),
                pltpu.VMEM((f, width), jnp.float32),
                pltpu.VMEM((f, width), jnp.float32),
                pltpu.VMEM((RADII, f, 2 * f), jnp.float32),
                pltpu.SMEM((1, RADII), jnp.int32),
                dma((3,)),
                dma((parts,)),
                dma((parts,)),
                dma((MATE_PIECES,)),
                dma((MATE_PIECES,)),
                dma((4,)),
                dma((4,)),
                dma((6,)),
                dma((10,)),
                pltpu.SemaphoreType.REGULAR,
                pltpu.SemaphoreType.REGULAR,
            ],
            compiler_params=pltpu.CompilerParams(collective_id=0, has_side_effects=True),
            name="two_time",
        )(frames, annulus_label, lag_width)

    return jax.shard_map(
        shards,
        mesh=mesh,
        in_specs=(P("pb", "tm", "pix"), P("pb", "pix"), P("pb", None)),
        out_specs=P("pb", None, "tm", "pix"),
        check_vma=False,
    )
```

```python
import functools

import jax
import jax.numpy as jnp
from jax import lax
from jax.experimental import pallas as pl
from jax.experimental.pallas import tpu as pltpu
from jax.sharding import PartitionSpec as P

MESH = pl.DeviceIdType.MESH
RADII = 4
CHUNK = 1024
MATE_PIECES = 4
ONES = 16


def pieces_of(pixels):
    late, first, width = [], 0, pixels // 2
    while width >= pixels // 64:
        late.append((1, first, width))
        first, width = first + width, width // 2
    early = [(0, 0, pixels)]
    return early, late + [(1, first, pixels - first)]


def over_half(masks, rows):
    groups = rows.reshape(1, -1, 16, rows.shape[-1])
    return (groups * masks[:, None]).reshape(-1, rows.shape[-1])


def over_rows(masks, block):
    groups = block.reshape(2, 1, -1, 16, block.shape[-1])
    return (groups * masks[None, :, None]).reshape(-1, block.shape[-1])


def contract(rows, columns):
    return lax.dot_general(rows, columns, (((1,), (1,)), ((), ())), preferred_element_type=jnp.float32)


def joined(left, right, radius, skew):
    width = left.shape[1] // 2
    quarter = width // RADII
    shape = (left.shape[0], width)
    place = lax.broadcasted_iota(jnp.int32, shape, 1)
    if skew:
        place = (place + lax.broadcasted_iota(jnp.int32, shape, 0)) & (width - 1)
    result = None
    for i in range(4):
        piece = (left, right)[i // 2][:, i % 2 * width : (i % 2 + 1) * width]
        lanes = (place + (radius - i) % 4 * quarter) & (width - 1)
        piece = jnp.take_along_axis(piece, lanes, axis=1)
        result = piece if result is None else jnp.where(place < i * quarter, result, piece)
    return result


def needed(f, half, below):
    if below:
        return (0, f) if half == 0 else (f // 2, f)
    return (0, f // 2) if half == 0 else (0, f)


def kernel(
    n,
    annulus_size,
    frames_ref,
    label_ref,
    lag_ref,
    out_ref,
    ab,
    stream,
    label,
    mask,
    acc1,
    acc2,
    from_pix,
    sums,
    low,
    high,
    from_even,
    from_even_x0,
    from_next_low,
    from_next_high,
    left,
    right,
    weight,
    widths,
    own_sem,
    stream_send,
    stream_recv,
    mate_send,
    mate_recv,
    early_send,
    early_recv,
    late_send,
    late_recv,
    extended,
    known,
):
    f, pixels = frames_ref.shape[1:]
    early_pieces, late_pieces = pieces_of(pixels)
    chunk = min(CHUNK, pixels // 32)
    chunks, per_piece = pixels // chunk, pixels // chunk // MATE_PIECES
    h = f // 2
    tiles = (slice(0, RADII * h), slice(RADII * h, RADII * f))
    own_rows, mate_rows = slice(ONES, ONES + f), slice(ONES + f, ONES + 2 * f)

    me, x = lax.axis_index("tm"), lax.axis_index("pix")
    odd = lax.rem(me, 2)
    even = odd == 0
    mate = me + 1 - 2 * odd
    ahead, behind = lax.rem(me + 2, n), lax.rem(me + n - 2, n)
    target = lax.rem(me + n - 2 + 4 * odd, n)
    source = lax.rem(me + n + 2 - 4 * odd, n)
    has_behind, has_ahead = me >= 2, me < n - 2
    sends = (even & has_behind) | ((odd == 1) & has_ahead)
    receives = (even & has_ahead) | ((odd == 1) & has_behind)
    other = 1 - x

    def at(k, count=1):
        return pl.ds(pl.multiple_of(k * chunk, chunk), chunk * count)

    def send(src, dst, sems, tm, pix):
        return pltpu.make_async_remote_copy(
            src_ref=src, dst_ref=dst, send_sem=sems[0], recv_sem=sems[1], device_id={"tm": tm, "pix": pix}, device_id_type=MESH
        )

    stream_copies = [
        send(
            frames_ref.at[0, half * h : (half + 1) * h, pl.ds(first, width)],
            stream.at[half * h : (half + 1) * h, pl.ds(first, width)],
            (stream_send.at[i], stream_recv.at[i]),
            target,
            x,
        )
        for i, (half, first, width) in enumerate(early_pieces + late_pieces)
    ]
    early_copies, late_copies = stream_copies[: len(early_pieces)], stream_copies[len(early_pieces) :]

    def mate_copy(k):
        columns = at(k * per_piece, per_piece)
        return send(frames_ref.at[0, :, columns], ab.at[mate_rows, columns], (mate_send.at[k], mate_recv.at[k]), mate, x)

    own_copy = pltpu.make_async_copy(frames_ref.at[0], ab.at[own_rows], own_sem.at[0])
    label_copy = pltpu.make_async_copy(label_ref, label, own_sem.at[1])
    lag_copy = pltpu.make_async_copy(lag_ref, widths, own_sem.at[2])

    def early(i):
        return early_send.at[i], early_recv.at[i]

    def late(i):
        return late_send.at[i], late_recv.at[i]

    pix_copies = [send(acc1.at[i], from_pix.at[i], early(i), me, other) for i in range(2)]
    sums_back = send(sums.at[0], sums.at[2], early(2), behind, x)
    sums_mate_odd = send(sums.at[0], sums.at[1], early(3), mate, x)
    sums_mate_even = send(sums.at[2], sums.at[1], early(3), mate, x)
    def tile_copies(base, dst, below, way, arrival, tm, pix):
        copies = []
        for half in range(2):
            start, stop = needed(f, half, below)
            src = acc2.at[half, base + start : base + stop]
            sems = (late_send.at[way + half], late_recv.at[arrival + half])
            copies.append(send(src, dst.at[half, start:stop], sems, tm, pix))
        return copies

    ac_copies = tile_copies(0, from_even_x0, True, 0, 0, me, 1)
    bc_copies = [
        [tile_copies(f, from_even.at[i], j == 0, 2 + 2 * j, 2 + 2 * i, mate, j) for j in range(2)] for i in range(2)
    ]

    def bd_copies(x_from):
        return [
            send(src, dst.at[x_from], (late_send.at[i], late_recv.at[6 + 2 * x_from + i]), behind, 1)
            for i, (src, dst) in enumerate(((low, from_next_low), (high, from_next_high)))
        ]

    def exchange(half):
        @pl.when(even & (x == 0))
        def _():
            each([bc_copies[0][1][half], ac_copies[half], bc_copies[0][0][half]], "start")

        @pl.when(even & (x == 1))
        def _():
            each([bc_copies[1][0][half], bc_copies[1][1][half]], "start")

        if half == 1:

            @pl.when((odd == 1) & has_behind)
            def _():
                each(bd_copies(x)[::-1], "start")

    def gather(half):
        below, above = slice(*needed(f, half, True)), slice(*needed(f, half, False))

        @pl.when(even & (x == 1))
        def _():
            ac_copies[half].wait_recv()
            right[below, tiles[half]] = acc2[half, below] + from_even_x0[half, below]

        @pl.when((odd == 1) & (x == 0))
        def _():
            each([bc_copies[0][0][half], bc_copies[1][0][half]], "wait_recv")
            right[below, tiles[half]] = from_even[0, half, below] + from_even[1, half, below]

        @pl.when((odd == 1) & (x == 1))
        def _():
            each([bc_copies[0][1][half], bc_copies[1][1][half]], "wait_recv")
            left[above, tiles[half]] = from_even[0, half, above] + from_even[1, half, above]

        if half == 1:

            @pl.when((odd == 1) & (x == 1) & has_ahead)
            def _():
                each(bd_copies(0) + bd_copies(1), "wait_recv")
                right[0:h, tiles[0]] = from_next_low[0] + from_next_low[1]
                right[h:f] = from_next_high[0] + from_next_high[1]

    def each(copies, action):
        for copy in copies:
            getattr(copy, action)()

    def signal(semaphore, tm, pix):
        pl.semaphore_signal(semaphore, inc=1, device_id={"tm": tm, "pix": pix}, device_id_type=MESH)

    def one_if(condition):
        return jnp.where(condition, 1, 0).astype(jnp.int32)

    label_copy.start()
    own_copy.start()
    lag_copy.start()

    barrier = pltpu.get_barrier_semaphore()

    @pl.when(receives)
    def _():
        signal(barrier, source, x)

    signal(barrier, mate, x)
    signal(barrier, me, other)
    pl.semaphore_wait(barrier, 2 + one_if(sends))

    @pl.when(sends)
    def _():
        each(early_copies, "start")
        signal(known, target, x)

    @pl.when(odd == 1)
    def _():
        @pl.loop(0, MATE_PIECES)
        def _(k):
            mate_copy(k).start()

    @pl.when(~has_ahead)
    def _():
        sums[2] = jnp.zeros_like(sums[2])

    acc1[...] = jnp.zeros_like(acc1)
    for tile in (acc2, low, high, left, right):
        tile[...] = jnp.zeros_like(tile)

    ab[0:ONES, :] = jnp.ones((ONES, pixels), jnp.bfloat16)
    label_copy.wait()

    @pl.loop(0, chunks)
    def _(k):
        labels = jnp.broadcast_to(label[:, at(k)], (16, chunk))
        for a in range(RADII):
            mask[a, :, at(k)] = jnp.where(labels == a, 1.0, 0.0).astype(jnp.bfloat16)

    own_copy.wait()

    @pl.loop(0, chunks)
    def _(k):
        masks = mask[:, :, at(k)]
        acc1[0] += contract(ab[0 : ONES + f, at(k)], over_rows(masks, ab[own_rows, at(k)]))

    pix_copies[0].start()

    @pl.when(receives)
    def _():
        pl.semaphore_wait(known, 1)

    signal(extended, mate, x)
    signal(extended, me, other)

    @pl.when(even)
    def _():
        @pl.loop(0, MATE_PIECES)
        def _(piece):
            mate_copy(piece).wait_recv()

            @pl.loop(piece * per_piece, piece * per_piece + per_piece)
            def _(k):
                masks = mask[:, :, at(k)]
                acc1[1] += contract(ab[0 : ONES + f, at(k)], over_rows(masks, ab[mate_rows, at(k)]))

        pix_copies[1].start()

    pix_copies[0].wait()
    sums[0] = acc1[0, 0:8] + from_pix[0, 0:8]

    @pl.when(has_behind)
    def _():
        sums_back.start()

    @pl.when(odd == 1)
    def _():
        sums_mate_odd.start()

    @pl.when(sends)
    def _():
        each(late_copies, "start")

    def multiply(half, columns):
        rows = slice(half * h, (half + 1) * h)

        @pl.when(even)
        def _():
            spread = over_half(mask[:, :, columns], stream[rows, columns])
            first = needed(f, half, True)[0]
            acc2[half, first : 2 * f] += contract(ab[ONES + first : ONES + 2 * f, columns], spread)

        @pl.when(odd == 1)
        def _():
            if half == 0:
                spread = over_half(mask[:, :, columns], ab[ONES : ONES + h, columns])
                low[...] += contract(stream[rows, columns], spread)
            else:
                spread = over_rows(mask[:, :, columns], ab[own_rows, columns])
                high[...] += contract(stream[rows, columns], spread)

    def multiply_all(copies, pieces):
        @pl.when(receives)
        def _():
            for copy, (half, first, width) in zip(copies, pieces):
                copy.wait_recv()
                step = min(chunk, width)

                @pl.loop(0, width // step)
                def _(k, half=half, first=first, step=step):
                    multiply(half, pl.ds(pl.multiple_of(first + k * step, step), step))

    multiply_all(early_copies, early_pieces)
    pl.semaphore_wait(extended, 2)
    exchange(0)

    @pl.when(has_ahead)
    def _():
        sums_back.wait_recv()

    @pl.when(has_behind)
    def _():
        sums_back.wait_send()

    @pl.when(even)
    def _():
        sums_mate_even.start()
        pix_copies[1].wait()
        sums_mate_even.wait()

    @pl.when(odd == 1)
    def _():
        sums_mate_odd.wait()

    lag_copy.wait()
    row = lax.broadcasted_iota(jnp.int32, (f, 2 * f), 0)
    lane = lax.broadcasted_iota(jnp.int32, (f, 2 * f), 1)
    lag = x * f + lane
    inside = me * f + row + lag < n * f
    near, far = sums[x, 0:1], sums[x + 1, 0:1]
    wide = (f, RADII * f)
    for a in range(RADII):
        own = joined(sums[0], sums[0], a, False)[0:1]
        own = jnp.sum(jnp.where(row == lane, jnp.broadcast_to(own, (f, 2 * f)), 0.0), axis=1, keepdims=True)
        there = joined(jnp.broadcast_to(near, wide), jnp.broadcast_to(far, wide), a, True)
        valid = (lag < widths[0, a]) & inside
        weight[a] = jnp.where(valid, annulus_size / (own * there), 0.0)

    @pl.when(even & (x == 0))
    def _():
        left[...] = acc1[0, own_rows] + from_pix[0, own_rows]
        right[...] = acc1[1, own_rows] + from_pix[1, own_rows]

    @pl.when(even & (x == 1))
    def _():
        left[...] = acc1[1, own_rows] + from_pix[1, own_rows]

    @pl.when((odd == 1) & (x == 0))
    def _():
        left[...] = acc1[0, own_rows] + from_pix[0, own_rows]

    multiply_all(late_copies[:1], late_pieces[:1])
    gather(0)

    def finish():
        for a in range(RADII):
            out_ref[0, a] = (joined(left[...], right[...], a, True) * weight[a])[:, 0:f]

    @pl.when(even | (x == 0))
    def _():
        finish()

    multiply_all(late_copies[1:], late_pieces[1:])
    exchange(1)
    gather(1)

    @pl.when((odd == 1) & (x == 1))
    def _():
        finish()

    @pl.when(odd + x == 1)
    def _():
        place = lax.broadcasted_iota(jnp.int32, (f, 2 * f), 0) + lax.broadcasted_iota(jnp.int32, (f, 2 * f), 1)
        last = right[:, tiles[1]]
        for a in range(RADII):
            lanes = (place + (a + 1) % 4 * h) & (2 * f - 1)
            patch = (jnp.take_along_axis(last, lanes, axis=1) * weight[a])[:, 0:f]
            out_ref[0, a] = jnp.where(place[:, 0:f] < 3 * h, out_ref[0, a], patch)

    @pl.when(sends)
    def _():
        each(stream_copies, "wait_send")

    @pl.when(odd == 1)
    def _():
        @pl.loop(0, MATE_PIECES)
        def _(k):
            mate_copy(k).wait_send()

        @pl.when(has_behind)
        def _():
            each(bd_copies(x), "wait_send")

    @pl.when(even)
    def _():
        for i in range(2):

            @pl.when(x == i)
            def _(i=i):
                each(bc_copies[i][0] + bc_copies[i][1], "wait_send")

        @pl.when(x == 0)
        def _():
            each(ac_copies, "wait_send")


def solution(mesh):
    n = mesh.shape["tm"]

    def shards(frames, annulus_label, lag_width):
        _, f, pixels = frames.shape
        parts = sum(map(len, pieces_of(pixels)))
        h = f // 2
        annulus_size = pixels * mesh.shape["pix"] // RADII
        width = RADII * f
        any_space = pl.BlockSpec(memory_space=pl.ANY)
        dma = pltpu.SemaphoreType.DMA
        return pl.pallas_call(
            functools.partial(kernel, n, float(annulus_size)),
            out_shape=pltpu.VMEM((1, RADII, f, f), jnp.float32),
            in_specs=[any_space] * 3,
            out_specs=pl.BlockSpec(memory_space=pltpu.VMEM),
            scratch_shapes=[
                pltpu.VMEM((ONES + 2 * f, pixels), jnp.bfloat16),
                pltpu.VMEM((f, pixels), jnp.bfloat16),
                pltpu.VMEM((1, pixels), jnp.int32),
                pltpu.VMEM((RADII, 16, pixels), jnp.bfloat16),
                pltpu.VMEM((2, ONES + f, width), jnp.float32),
                pltpu.VMEM((2, 2 * f, width // 2), jnp.float32),
                pltpu.VMEM((2, ONES + f, width), jnp.float32),
                pltpu.VMEM((3, 8, width), jnp.float32),
                pltpu.VMEM((h, width // 2), jnp.float32),
                pltpu.VMEM((h, width), jnp.float32),
                pltpu.VMEM((2, 2, f, width // 2), jnp.float32),
                pltpu.VMEM((2, f, width // 2), jnp.float32),
                pltpu.VMEM((2, h, width // 2), jnp.float32),
                pltpu.VMEM((2, h, width), jnp.float32),
                pltpu.VMEM((f, width), jnp.float32),
                pltpu.VMEM((f, width), jnp.float32),
                pltpu.VMEM((RADII, f, 2 * f), jnp.float32),
                pltpu.SMEM((1, RADII), jnp.int32),
                dma((3,)),
                dma((parts,)),
                dma((parts,)),
                dma((MATE_PIECES,)),
                dma((MATE_PIECES,)),
                dma((4,)),
                dma((4,)),
                dma((6,)),
                dma((10,)),
                pltpu.SemaphoreType.REGULAR,
                pltpu.SemaphoreType.REGULAR,
            ],
            compiler_params=pltpu.CompilerParams(collective_id=0, has_side_effects=True),
            name="two_time",
        )(frames, annulus_label, lag_width)

    return jax.shard_map(
        shards,
        mesh=mesh,
        in_specs=(P("pb", "tm", "pix"), P("pb", "pix"), P("pb", None)),
        out_specs=P("pb", None, "tm", "pix"),
        check_vma=False,
    )
```

```python
import functools

import jax
import jax.numpy as jnp
from jax import lax
from jax.experimental import pallas as pl
from jax.experimental.pallas import tpu as pltpu
from jax.sharding import PartitionSpec as P

MESH = pl.DeviceIdType.MESH
RADII = 4
CHUNK = 1024
MATE_PIECES = 4
ONES = 16


def pieces_of(pixels):
    late, first, width = [], 0, pixels // 2
    while width >= pixels // 64:
        late.append((1, first, width))
        first, width = first + width, width // 2
    early = [(0, 0, pixels)]
    return early, late + [(1, first, pixels - first)]


def over_half(masks, rows):
    groups = rows.reshape(1, -1, 16, rows.shape[-1])
    return (groups * masks[:, None]).reshape(-1, rows.shape[-1])


def over_rows(masks, block):
    groups = block.reshape(2, 1, -1, 16, block.shape[-1])
    return (groups * masks[None, :, None]).reshape(-1, block.shape[-1])


def contract(rows, columns):
    return lax.dot_general(rows, columns, (((1,), (1,)), ((), ())), preferred_element_type=jnp.float32)


def joined(left, right, radius, skew):
    width = left.shape[1] // 2
    quarter = width // RADII
    shape = (left.shape[0], width)
    place = lax.broadcasted_iota(jnp.int32, shape, 1)
    if skew:
        place = (place + lax.broadcasted_iota(jnp.int32, shape, 0)) & (width - 1)
    result = None
    for i in range(4):
        piece = (left, right)[i // 2][:, i % 2 * width : (i % 2 + 1) * width]
        lanes = (place + (radius - i) % 4 * quarter) & (width - 1)
        piece = jnp.take_along_axis(piece, lanes, axis=1)
        result = piece if result is None else jnp.where(place < i * quarter, result, piece)
    return result


def needed(f, half, below):
    if below:
        return (0, f) if half == 0 else (f // 2, f)
    return (0, f // 2) if half == 0 else (0, f)


def kernel(
    n,
    annulus_size,
    frames_ref,
    label_ref,
    lag_ref,
    out_ref,
    ab,
    stream,
    label,
    mask,
    acc1,
    acc2,
    from_pix,
    sums,
    low,
    high,
    from_even,
    from_even_x0,
    from_next_low,
    from_next_high,
    left,
    right,
    weight,
    widths,
    own_sem,
    stream_send,
    stream_recv,
    mate_send,
    mate_recv,
    early_send,
    early_recv,
    late_send,
    late_recv,
    extended,
    known,
):
    f, pixels = frames_ref.shape[1:]
    early_pieces, late_pieces = pieces_of(pixels)
    chunk = min(CHUNK, pixels // 32)
    chunks, per_piece = pixels // chunk, pixels // chunk // MATE_PIECES
    h = f // 2
    tiles = (slice(0, RADII * h), slice(RADII * h, RADII * f))
    own_rows, mate_rows = slice(ONES, ONES + f), slice(ONES + f, ONES + 2 * f)

    me, x = lax.axis_index("tm"), lax.axis_index("pix")
    odd = lax.rem(me, 2)
    even = odd == 0
    mate = me + 1 - 2 * odd
    ahead, behind = lax.rem(me + 2, n), lax.rem(me + n - 2, n)
    target = lax.rem(me + n - 2 + 4 * odd, n)
    source = lax.rem(me + n + 2 - 4 * odd, n)
    has_behind, has_ahead = me >= 2, me < n - 2
    sends = (even & has_behind) | ((odd == 1) & has_ahead)
    receives = (even & has_ahead) | ((odd == 1) & has_behind)
    other = 1 - x

    def at(k, count=1):
        return pl.ds(pl.multiple_of(k * chunk, chunk), chunk * count)

    def send(src, dst, sems, tm, pix):
        return pltpu.make_async_remote_copy(
            src_ref=src, dst_ref=dst, send_sem=sems[0], recv_sem=sems[1], device_id={"tm": tm, "pix": pix}, device_id_type=MESH
        )

    stream_copies = [
        send(
            frames_ref.at[0, half * h : (half + 1) * h, pl.ds(first, width)],
            stream.at[half * h : (half + 1) * h, pl.ds(first, width)],
            (stream_send.at[i], stream_recv.at[i]),
            target,
            x,
        )
        for i, (half, first, width) in enumerate(early_pieces + late_pieces)
    ]
    early_copies, late_copies = stream_copies[: len(early_pieces)], stream_copies[len(early_pieces) :]

    def mate_copy(k):
        columns = at(k * per_piece, per_piece)
        return send(frames_ref.at[0, :, columns], ab.at[mate_rows, columns], (mate_send.at[k], mate_recv.at[k]), mate, x)

    own_copy = pltpu.make_async_copy(frames_ref.at[0], ab.at[own_rows], own_sem.at[0])
    label_copy = pltpu.make_async_copy(label_ref, label, own_sem.at[1])
    lag_copy = pltpu.make_async_copy(lag_ref, widths, own_sem.at[2])

    def early(i):
        return early_send.at[i], early_recv.at[i]

    def late(i):
        return late_send.at[i], late_recv.at[i]

    pix_copies = [send(acc1.at[i], from_pix.at[i], early(i), me, other) for i in range(2)]
    sums_back = send(sums.at[0], sums.at[2], early(2), behind, x)
    sums_mate_odd = send(sums.at[0], sums.at[1], early(3), mate, x)
    sums_mate_even = send(sums.at[2], sums.at[1], early(3), mate, x)
    def tile_copies(base, dst, below, way, arrival, tm, pix):
        copies = []
        for half in range(2):
            start, stop = needed(f, half, below)
            src = acc2.at[half, base + start : base + stop]
            sems = (late_send.at[way + half], late_recv.at[arrival + half])
            copies.append(send(src, dst.at[half, start:stop], sems, tm, pix))
        return copies

    ac_copies = tile_copies(0, from_even_x0, True, 0, 0, me, 1)
    bc_copies = [
        [tile_copies(f, from_even.at[i], j == 0, 2 + 2 * j, 2 + 2 * i, mate, j) for j in range(2)] for i in range(2)
    ]

    def bd_copies(x_from):
        return [
            send(src, dst.at[x_from], (late_send.at[i], late_recv.at[6 + 2 * x_from + i]), behind, 1)
            for i, (src, dst) in enumerate(((low, from_next_low), (high, from_next_high)))
        ]

    def exchange(half):
        @pl.when(even & (x == 0))
        def _():
            each([bc_copies[0][1][0]] if half == 0 else [], "start")
            each([ac_copies[half], bc_copies[0][0][half]], "start")

        @pl.when(even & (x == 1))
        def _():
            each([bc_copies[1][0][0]] if half == 0 else [], "start")
            bc_copies[1][1][half].start()

        if half == 1:

            @pl.when((odd == 1) & has_behind)
            def _():
                each(bd_copies(x)[::-1], "start")

    def gather(half):
        below, above = slice(*needed(f, half, True)), slice(*needed(f, half, False))

        @pl.when(even & (x == 1))
        def _():
            ac_copies[half].wait_recv()
            right[below, tiles[half]] = acc2[half, below] + from_even_x0[half, below]

        @pl.when((odd == 1) & (x == 0))
        def _():
            each([bc_copies[0][0][half], bc_copies[1][0][half]], "wait_recv")
            right[below, tiles[half]] = from_even[0, half, below] + from_even[1, half, below]

        @pl.when((odd == 1) & (x == 1))
        def _():
            each([bc_copies[0][1][half], bc_copies[1][1][half]], "wait_recv")
            left[above, tiles[half]] = from_even[0, half, above] + from_even[1, half, above]

        if half == 1:

            @pl.when((odd == 1) & (x == 1) & has_ahead)
            def _():
                each(bd_copies(0) + bd_copies(1), "wait_recv")
                right[0:h, tiles[0]] = from_next_low[0] + from_next_low[1]
                right[h:f] = from_next_high[0] + from_next_high[1]

    def each(copies, action):
        for copy in copies:
            getattr(copy, action)()

    def signal(semaphore, tm, pix):
        pl.semaphore_signal(semaphore, inc=1, device_id={"tm": tm, "pix": pix}, device_id_type=MESH)

    def one_if(condition):
        return jnp.where(condition, 1, 0).astype(jnp.int32)

    label_copy.start()
    own_copy.start()
    lag_copy.start()

    barrier = pltpu.get_barrier_semaphore()

    @pl.when(receives)
    def _():
        signal(barrier, source, x)

    signal(barrier, mate, x)
    signal(barrier, me, other)
    pl.semaphore_wait(barrier, 2 + one_if(sends))

    @pl.when(sends)
    def _():
        each(early_copies, "start")
        signal(known, target, x)

    @pl.when(odd == 1)
    def _():
        @pl.loop(0, MATE_PIECES)
        def _(k):
            mate_copy(k).start()

    @pl.when(~has_ahead)
    def _():
        sums[2] = jnp.zeros_like(sums[2])

    acc1[...] = jnp.zeros_like(acc1)
    for tile in (acc2, low, high, left, right):
        tile[...] = jnp.zeros_like(tile)

    ab[0:ONES, :] = jnp.ones((ONES, pixels), jnp.bfloat16)
    label_copy.wait()

    @pl.loop(0, chunks)
    def _(k):
        labels = jnp.broadcast_to(label[:, at(k)], (16, chunk))
        for a in range(RADII):
            mask[a, :, at(k)] = jnp.where(labels == a, 1.0, 0.0).astype(jnp.bfloat16)

    own_copy.wait()

    @pl.loop(0, chunks)
    def _(k):
        masks = mask[:, :, at(k)]
        acc1[0] += contract(ab[0 : ONES + f, at(k)], over_rows(masks, ab[own_rows, at(k)]))

    pix_copies[0].start()

    @pl.when(receives)
    def _():
        pl.semaphore_wait(known, 1)

    signal(extended, mate, x)
    signal(extended, me, other)

    @pl.when(even)
    def _():
        @pl.loop(0, MATE_PIECES)
        def _(piece):
            mate_copy(piece).wait_recv()

            @pl.loop(piece * per_piece, piece * per_piece + per_piece)
            def _(k):
                masks = mask[:, :, at(k)]
                acc1[1] += contract(ab[0 : ONES + f, at(k)], over_rows(masks, ab[mate_rows, at(k)]))

        pix_copies[1].start()

    pix_copies[0].wait()
    sums[0] = acc1[0, 0:8] + from_pix[0, 0:8]

    @pl.when(has_behind)
    def _():
        sums_back.start()

    @pl.when(odd == 1)
    def _():
        sums_mate_odd.start()

    @pl.when(sends)
    def _():
        each(late_copies, "start")

    def multiply(half, columns):
        rows = slice(half * h, (half + 1) * h)

        @pl.when(even)
        def _():
            spread = over_half(mask[:, :, columns], stream[rows, columns])
            first = needed(f, half, True)[0]
            acc2[half, first : 2 * f] += contract(ab[ONES + first : ONES + 2 * f, columns], spread)

        @pl.when(odd == 1)
        def _():
            if half == 0:
                spread = over_half(mask[:, :, columns], ab[ONES : ONES + h, columns])
                low[...] += contract(stream[rows, columns], spread)
            else:
                spread = over_rows(mask[:, :, columns], ab[own_rows, columns])
                high[...] += contract(stream[rows, columns], spread)

    def multiply_all(copies, pieces):
        @pl.when(receives)
        def _():
            for copy, (half, first, width) in zip(copies, pieces):
                copy.wait_recv()
                step = min(chunk, width)

                @pl.loop(0, width // step)
                def _(k, half=half, first=first, step=step):
                    multiply(half, pl.ds(pl.multiple_of(first + k * step, step), step))

    multiply_all(early_copies, early_pieces)
    pl.semaphore_wait(extended, 2)
    exchange(0)

    @pl.when(has_ahead)
    def _():
        sums_back.wait_recv()

    @pl.when(has_behind)
    def _():
        sums_back.wait_send()

    @pl.when(even)
    def _():
        sums_mate_even.start()
        pix_copies[1].wait()
        sums_mate_even.wait()

    @pl.when(odd == 1)
    def _():
        sums_mate_odd.wait()

    lag_copy.wait()
    row = lax.broadcasted_iota(jnp.int32, (f, 2 * f), 0)
    lane = lax.broadcasted_iota(jnp.int32, (f, 2 * f), 1)
    lag = x * f + lane
    inside = me * f + row + lag < n * f
    near, far = sums[x, 0:1], sums[x + 1, 0:1]
    wide = (f, RADII * f)
    for a in range(RADII):
        own = joined(sums[0], sums[0], a, False)[0:1]
        own = jnp.sum(jnp.where(row == lane, jnp.broadcast_to(own, (f, 2 * f)), 0.0), axis=1, keepdims=True)
        there = joined(jnp.broadcast_to(near, wide), jnp.broadcast_to(far, wide), a, True)
        valid = (lag < widths[0, a]) & inside
        weight[a] = jnp.where(valid, annulus_size / (own * there), 0.0)

    @pl.when(even & (x == 0))
    def _():
        left[...] = acc1[0, own_rows] + from_pix[0, own_rows]
        right[...] = acc1[1, own_rows] + from_pix[1, own_rows]

    @pl.when(even & (x == 1))
    def _():
        left[...] = acc1[1, own_rows] + from_pix[1, own_rows]

    @pl.when((odd == 1) & (x == 0))
    def _():
        left[...] = acc1[0, own_rows] + from_pix[0, own_rows]

    multiply_all(late_copies[:1], late_pieces[:1])
    gather(0)

    def finish():
        for a in range(RADII):
            out_ref[0, a] = (joined(left[...], right[...], a, True) * weight[a])[:, 0:f]

    @pl.when(even | (x == 0))
    def _():
        finish()

    multiply_all(late_copies[1:-1], late_pieces[1:-1])
    _, final_first, final_width = late_pieces[-1]
    final = pl.ds(final_first, final_width)

    def multiply_rows(start, stop):
        @pl.when(receives & even)
        def _():
            spread = over_half(mask[:, :, final], stream[h:f, final])
            acc2[1, start:stop] += contract(ab[ONES + start : ONES + stop, final], spread)

    @pl.when(receives)
    def _():
        late_copies[-1].wait_recv()

    @pl.when(receives & (odd == 1))
    def _():
        multiply(1, final)

    multiply_rows(f, 2 * f)

    @pl.when(even & (x == 0))
    def _():
        bc_copies[0][1][1].start()

    @pl.when(even & (x == 1))
    def _():
        bc_copies[1][0][1].start()

    multiply_rows(h, f)
    exchange(1)
    gather(1)

    @pl.when((odd == 1) & (x == 1))
    def _():
        finish()

    @pl.when(odd + x == 1)
    def _():
        place = lax.broadcasted_iota(jnp.int32, (f, 2 * f), 0) + lax.broadcasted_iota(jnp.int32, (f, 2 * f), 1)
        last = right[:, tiles[1]]
        for a in range(RADII):
            lanes = (place + (a + 1) % 4 * h) & (2 * f - 1)
            patch = (jnp.take_along_axis(last, lanes, axis=1) * weight[a])[:, 0:f]
            out_ref[0, a] = jnp.where(place[:, 0:f] < 3 * h, out_ref[0, a], patch)

    @pl.when(sends)
    def _():
        each(stream_copies, "wait_send")

    @pl.when(odd == 1)
    def _():
        @pl.loop(0, MATE_PIECES)
        def _(k):
            mate_copy(k).wait_send()

        @pl.when(has_behind)
        def _():
            each(bd_copies(x), "wait_send")

    @pl.when(even)
    def _():
        for i in range(2):

            @pl.when(x == i)
            def _(i=i):
                each(bc_copies[i][0] + bc_copies[i][1], "wait_send")

        @pl.when(x == 0)
        def _():
            each(ac_copies, "wait_send")


def solution(mesh):
    n = mesh.shape["tm"]

    def shards(frames, annulus_label, lag_width):
        _, f, pixels = frames.shape
        parts = sum(map(len, pieces_of(pixels)))
        h = f // 2
        annulus_size = pixels * mesh.shape["pix"] // RADII
        width = RADII * f
        any_space = pl.BlockSpec(memory_space=pl.ANY)
        dma = pltpu.SemaphoreType.DMA
        return pl.pallas_call(
            functools.partial(kernel, n, float(annulus_size)),
            out_shape=pltpu.VMEM((1, RADII, f, f), jnp.float32),
            in_specs=[any_space] * 3,
            out_specs=pl.BlockSpec(memory_space=pltpu.VMEM),
            scratch_shapes=[
                pltpu.VMEM((ONES + 2 * f, pixels), jnp.bfloat16),
                pltpu.VMEM((f, pixels), jnp.bfloat16),
                pltpu.VMEM((1, pixels), jnp.int32),
                pltpu.VMEM((RADII, 16, pixels), jnp.bfloat16),
                pltpu.VMEM((2, ONES + f, width), jnp.float32),
                pltpu.VMEM((2, 2 * f, width // 2), jnp.float32),
                pltpu.VMEM((2, ONES + f, width), jnp.float32),
                pltpu.VMEM((3, 8, width), jnp.float32),
                pltpu.VMEM((h, width // 2), jnp.float32),
                pltpu.VMEM((h, width), jnp.float32),
                pltpu.VMEM((2, 2, f, width // 2), jnp.float32),
                pltpu.VMEM((2, f, width // 2), jnp.float32),
                pltpu.VMEM((2, h, width // 2), jnp.float32),
                pltpu.VMEM((2, h, width), jnp.float32),
                pltpu.VMEM((f, width), jnp.float32),
                pltpu.VMEM((f, width), jnp.float32),
                pltpu.VMEM((RADII, f, 2 * f), jnp.float32),
                pltpu.SMEM((1, RADII), jnp.int32),
                dma((3,)),
                dma((parts,)),
                dma((parts,)),
                dma((MATE_PIECES,)),
                dma((MATE_PIECES,)),
                dma((4,)),
                dma((4,)),
                dma((6,)),
                dma((10,)),
                pltpu.SemaphoreType.REGULAR,
                pltpu.SemaphoreType.REGULAR,
            ],
            compiler_params=pltpu.CompilerParams(collective_id=0, has_side_effects=True),
            name="two_time",
        )(frames, annulus_label, lag_width)

    return jax.shard_map(
        shards,
        mesh=mesh,
        in_specs=(P("pb", "tm", "pix"), P("pb", "pix"), P("pb", None)),
        out_specs=P("pb", None, "tm", "pix"),
        check_vma=False,
    )
```
